256 devices in a mesh: gx: 16 (over y, z_hi), gy: 4 (over x), gz: 4 (over z_lo, core).
Axes of the slice: x: 4, y: 4, z: 8 (z_hi: 4, z_lo: 2; z = z_hi * 2 + z_lo), core: 2. Of those that a mesh axis runs over, the one named last changes fastest.
Arguments:
- fields: float32 [6, 256, 64, 512], P(None, 'gx', 'gy', 'gz'), may hold values from -6 to 6
- polarization: float32 [6, 256, 64, 512], P(None, 'gx', 'gy', 'gz'), may hold values from -3 to 3
- material: int32 [256, 64, 512], P('gx', 'gy', 'gz'), may hold values from 0 to 4
- omega0: float32 [4], replicated, may hold values from 0.1 to 0.5
- damping: float32 [4], replicated, may hold values from 0.05 to 0.8
- strength: float32 [4], replicated, may hold values from 0.5 to 2.5
- tile_count: int32 [64, 4], P(('gx', 'gy')), may hold values from 1 to 18, 24 in all within a row
- tile_place: int32 [64, 4, 18], P(('gx', 'gy')), may hold values from 0 to 31, as said below
- dir_angles: float32 [2, 8192], replicated, may hold values from 0 to 3.14159
- dir_order: int32 [8192], replicated, may hold values from 0 to 8191, each once
Outputs:
- fields_out: float32 [6, 256, 64, 512], P(None, 'gx', 'gy', 'gz')
- far_field: float32 [8192, 8], P(('gx', 'gy', 'gz'))
The draws below stay inside these ranges and needn't reach their ends.
Inputs may be any that keep to these rules, and one draw needn't show every extreme that they name: `tile_count`: for each column g, the 4 counts sum to 24, and the largest of them is exactly 18. `tile_place`: the 18 positions of one device are distinct; only the first tile_count of them are live tiles.
All inputs are finite; a program needn't handle non-finite values.
Results may differ from the reference program's by a relative error of at most 0.0032.
Values may be sent and summed in bfloat16 or wider, within the bound.
No kernel may reach another device: no remote copies, remote signals or barrier semaphores. Data moves between devices by JAX's collectives and lax.ppermute only.
A program may use at most 64 MiB of HBM per device.

```python
import math
import jax
import jax.numpy as jnp
import numpy as np
from jax import lax

CX = 16
CY = 16
CZ = 128
TY = 8
MATS = 4
STEPS = 4
DIRS = 8192
TILE_MEAN = 6
TILE_MOST = 18
NX = 256
NY = 64
NZ = 512
GROUPS = 64
GROUP_TILES = 24
TILES_ALL = 1536
N_GY = 4
N_GZ = 4


def draw_tile_place(key, part):
    positions = CX * (CY // TY)
    layers = GROUP_TILES // TILE_MEAN
    row_total = GROUPS * layers
    scores = jax.random.randint(key, (row_total, positions), 0, 1 << 16) * positions + jnp.arange(positions)[None, :]
    chosen = jnp.argsort(scores, axis=1)[:, :TILE_MOST]
    return chosen.reshape(GROUPS, layers, TILE_MOST).astype(jnp.int32)


def set_ends(array, own_key, low, top_value):
    dims = array.shape
    spot = [jax.random.randint(jax.random.fold_in(own_key, axis), (), 0, dims[axis]) for axis in range(len(dims))]
    array = array.at[tuple(spot)].set(low)
    longest = dims.index(max(dims))
    spot[longest] = (spot[longest] + 1) % dims[longest]
    return array.at[tuple(spot)].set(top_value)


def block_levels(key, shape, shards, least, top_value):
    gain, own = 1.0, jax.random.fold_in(key, 6)
    for dim, blocks in shards:
        steps = jnp.exp(jax.random.uniform(jax.random.fold_in(own, dim), (blocks,), jnp.float32, least / len(shards), top_value / len(shards)))
        gain = gain * jnp.repeat(steps, shape[dim] // blocks).reshape([-1 if axis == dim else 1 for axis in range(len(shape))])
    return gain


def split_up(count, total, reach, skew):
    weights = [(1 << 20) // math.isqrt(rank ** skew) + 1 for rank in range(2, count + 1)]
    spare, given = total - reach - (count - 1), [1] * (count - 1)
    while spare > 0:
        movable = [i for i in range(count - 1) if given[i] < reach]
        pool, left = sum([weights[i] for i in movable]), spare
        for i in movable:
            extra = min(reach - given[i], max(1, left * weights[i] // pool), spare)
            given[i] = given[i] + extra
            spare = spare - extra
    return np.array([reach] + given)


def ragged_sizes(stream_key, number_of, total, reach, slope):
    if number_of == 2:
        one = jax.random.randint(stream_key, (), max(1, total - reach), min(reach, total - 1) + 1)
        return jnp.stack([one, total - one])
    sizes = jnp.asarray(split_up(number_of, total, reach, slope), jnp.int32)
    pairs = (number_of - 1) // 2
    source_of, sink = sizes[1:1 + 2 * pairs:2], sizes[2:2 + 2 * pairs:2]
    margin = jnp.minimum(source_of - 1, reach - sink)
    shifted = jax.random.randint(jax.random.fold_in(stream_key, 1), (pairs,), 0, 1 << 20) % (margin + 1)
    sizes = sizes.at[1:1 + 2 * pairs:2].set(source_of - shifted).at[2:2 + 2 * pairs:2].set(sink + shifted)
    return sizes[jax.random.permutation(jax.random.fold_in(stream_key, 2), number_of)]


def bell_draw(key, shape, width, reach, shards=(), kind=jnp.bfloat16):
    entries = width * jax.random.normal(key, shape, jnp.float32)
    if shards:
        entries = entries * block_levels(key, shape, shards, -0.22, 0.18)
    return jnp.clip(entries, -reach, reach).astype(kind)


def setup_inputs(seed: int = 0) -> dict:
    seeds = jax.random.split(jax.random.key(seed), 11)
    return {
        "fields": bell_draw(seeds[0], (6, NX, NY, NZ), 1.0, 6.0, ((1, 16), (2, 4), (3, 4)), jnp.float32),
        "polarization": bell_draw(seeds[1], (6, NX, NY, NZ), 0.5, 3.0, ((1, 16), (2, 4), (3, 4)), jnp.float32),
        "material": set_ends(jax.random.randint(seeds[2], (NX, NY, NZ), 0, MATS + 1), jax.random.fold_in(seeds[2], 1), 0, MATS).astype(jnp.int32),
        "omega0": jnp.clip(jnp.exp(jax.random.uniform(seeds[3], (MATS,), jnp.float32, math.log(0.1), math.log(0.5))), 0.1, 0.5),
        "damping": jnp.clip(jnp.exp(jax.random.uniform(seeds[4], (MATS,), jnp.float32, math.log(0.05), math.log(0.8))), 0.05, 0.8),
        "strength": jnp.clip(jax.random.uniform(seeds[5], (MATS,), jnp.float32, 0.5, 2.5), 0.5, 2.5),
        "tile_count": jax.vmap(lambda own: ragged_sizes(own, N_GZ, GROUP_TILES, TILE_MOST, 2))(jax.random.split(seeds[6], GROUPS)).reshape((GROUPS, N_GZ)).astype(jnp.int32),
        "tile_place": draw_tile_place(jax.random.fold_in(seeds[10], 71), 0),
        "dir_angles": jnp.clip(jax.random.uniform(seeds[8], (2, DIRS), jnp.float32, 0.0, 3.14159), 0.0, 3.14159),
        "dir_order": jax.random.permutation(seeds[9], DIRS).astype(jnp.int32),
    }


SPEED = 0.5
WAVE = 0.35

def lorentz(omega0, damping, strength):
    denominator = 1.0 + 0.5 * damping
    square = omega0 * omega0
    return ((2.0 - square) / denominator, -(1.0 - 0.5 * damping) / denominator, strength * square / denominator)

def lookup(material, coef_table):
    result = jnp.zeros(material.shape, jnp.float32)
    for mat_index in range(coef_table.shape[0]):
        result = result + jnp.where(material == mat_index + 1, coef_table[mat_index], 0.0)
    return result

def ahead(values, axis_id):
    extent = values.shape[axis_id]
    padded = jnp.pad(values, [(0, 1) if other == axis_id else (0, 0) for other in range(values.ndim)])
    return lax.slice_in_dim(padded, 1, extent + 1, axis=axis_id)

def behind(values, axis_id):
    extent = values.shape[axis_id]
    padded = jnp.pad(values, [(1, 0) if other == axis_id else (0, 0) for other in range(values.ndim)])
    return lax.slice_in_dim(padded, 0, extent, axis=axis_id)

def magnetic_update(electric, magnetic):
    electric_x, electric_y, electric_z = (electric[0], electric[1], electric[2])
    magnetic_x = magnetic[0] - SPEED * (ahead(electric_z, 1) - electric_z - (ahead(electric_y, 2) - electric_y))
    magnetic_y = magnetic[1] - SPEED * (ahead(electric_x, 2) - electric_x - (ahead(electric_z, 0) - electric_z))
    magnetic_z = magnetic[2] - SPEED * (ahead(electric_y, 0) - electric_y - (ahead(electric_x, 1) - electric_x))
    return jnp.stack([magnetic_x, magnetic_y, magnetic_z])

def curl_back(magnetic):
    magnetic_x, magnetic_y, magnetic_z = (magnetic[0], magnetic[1], magnetic[2])
    curl_x = magnetic_z - behind(magnetic_z, 1) - (magnetic_y - behind(magnetic_y, 2))
    curl_y = magnetic_x - behind(magnetic_x, 2) - (magnetic_z - behind(magnetic_z, 0))
    curl_z = magnetic_y - behind(magnetic_y, 0) - (magnetic_x - behind(magnetic_x, 1))
    return jnp.stack([curl_x, curl_y, curl_z])

def far_block(currents, tile_x, tile_y, tile_z, directions, rows_y, depth_z):
    row_pos = jnp.arange(rows_y, dtype=jnp.float32)
    depth_pos = jnp.arange(depth_z, dtype=jnp.float32)
    phases = WAVE * (directions[1][None, None, :] * row_pos[:, None, None] + directions[2][None, None, :] * depth_pos[None, :, None])
    phase_table = jnp.concatenate([jnp.cos(phases), jnp.sin(phases)], axis=2).astype(jnp.bfloat16)
    block_width = directions.shape[1]
    phase_table = phase_table.reshape(rows_y * depth_z, 2 * block_width)
    tiles = currents.shape[0]
    products = jnp.dot(currents.reshape(tiles * 8, rows_y * depth_z).astype(jnp.float32), phase_table.astype(jnp.float32), precision=lax.Precision.HIGHEST)
    products = products.reshape(tiles, 4, 2, 2, block_width)
    real_part = products[:, :, 0, 0] - products[:, :, 1, 1]
    imag_part = products[:, :, 0, 1] + products[:, :, 1, 0]
    tile_phase = WAVE * (directions[0][None, :] * tile_x[:, None] + directions[1][None, :] * tile_y[:, None] + directions[2][None, :] * tile_z[:, None])
    tile_cos = jnp.cos(tile_phase)[:, None, :]
    tile_sin = jnp.sin(tile_phase)[:, None, :]
    far_real = lax.optimization_barrier(jnp.sum(real_part * tile_cos - imag_part * tile_sin, axis=0))
    far_imag = lax.optimization_barrier(jnp.sum(real_part * tile_sin + imag_part * tile_cos, axis=0))
    return jnp.stack([far_real, far_imag], axis=1).reshape(8, block_width)

def reference(fields, polarization, material, omega0, damping, strength, tile_count, tile_place, dir_angles, dir_order):
    table_a, table_b, table_c = lorentz(omega0, damping, strength)
    coef_a = lookup(material, table_a)
    coef_b = lookup(material, table_b)
    coef_c = lookup(material, table_c)
    sheet_mask = jnp.where(material > 0, 1.0, 0.0).astype(jnp.float32)
    electric = fields[0:3]
    magnetic = fields[3:6]
    pol_now = polarization[0:3]
    pol_old = polarization[3:6]
    empty_sum = jnp.zeros((2,) + material.shape, jnp.float32)
    ele_real, ele_imag, mag_real, mag_imag = (empty_sum, empty_sum, empty_sum, empty_sum)
    for instant in range(STEPS):
        magnetic = magnetic_update(electric, magnetic)
        saturation = 1.0 / (1.0 + electric[0] * electric[0] + electric[1] * electric[1] + electric[2] * electric[2])
        pol_new = coef_a * pol_now + coef_b * pol_old + coef_c * saturation * electric
        electric = electric + SPEED * curl_back(magnetic) - sheet_mask * (pol_new - pol_now)
        pol_old = pol_now
        pol_now = pol_new
        angle_h = WAVE * SPEED * (instant + 0.5)
        angle_e = WAVE * SPEED * (instant + 1.0)
        mag_real = mag_real + math.cos(angle_h) * magnetic[1:3]
        mag_imag = mag_imag - math.sin(angle_h) * magnetic[1:3]
        ele_real = ele_real + math.cos(angle_e) * electric[1:3]
        ele_imag = ele_imag - math.sin(angle_e) * electric[1:3]
    fields_out = jnp.concatenate([electric, magnetic], axis=0)
    currents = jnp.stack([-mag_real[1], -mag_imag[1], mag_real[0], mag_imag[0], ele_real[1], ele_imag[1], -ele_real[0], -ele_imag[0]])
    blocks_y = CY // TY
    run_ends = jnp.cumsum(tile_count, axis=1).astype(jnp.int32)
    starts = run_ends - tile_count
    rank_ids = jnp.arange(GROUP_TILES, dtype=jnp.int32)
    source = lax.optimization_barrier(jnp.sum((run_ends[:, None, :] <= rank_ids[None, :, None]).astype(jnp.int32), axis=2))
    within = rank_ids[None, :] - jnp.take_along_axis(starts, source, axis=1)
    group_ids = jnp.broadcast_to(jnp.arange(GROUPS, dtype=jnp.int32)[:, None], source.shape)
    places = tile_place[group_ids, source, within]
    tile_x = (group_ids // N_GY * CX + places // blocks_y).reshape(-1).astype(jnp.int32)
    tile_y = (group_ids % N_GY * CY + places % blocks_y * TY).reshape(-1).astype(jnp.int32)
    tile_z = (source * CZ).reshape(-1).astype(jnp.int32)

    def cut_patch(x_start, y_start, z_start):
        patch = lax.dynamic_slice(currents, (jnp.int32(0), x_start, y_start, z_start), (8, 1, TY, CZ))
        return patch.reshape(8, TY * CZ)
    patches = jax.vmap(cut_patch)(tile_x, tile_y, tile_z).astype(jnp.bfloat16)
    polar_angle = jnp.take(dir_angles[0], dir_order)
    azimuth = jnp.take(dir_angles[1], dir_order)
    dir_vec = jnp.stack([jnp.sin(polar_angle) * jnp.cos(azimuth), jnp.sin(polar_angle) * jnp.sin(azimuth), jnp.cos(polar_angle)])
    block_width = math.gcd(DIRS, 512)
    pos_x = tile_x.astype(jnp.float32)
    pos_y = tile_y.astype(jnp.float32)
    pos_z = tile_z.astype(jnp.float32)

    def block_far(offset):
        directions = lax.dynamic_slice_in_dim(dir_vec, offset, block_width, 1)
        return far_block(patches, pos_x, pos_y, pos_z, directions, TY, CZ)
    far_blocks = lax.map(block_far, jnp.arange(DIRS // block_width, dtype=jnp.int32) * block_width)
    norm_scale = 1.0 / math.sqrt(TILES_ALL * TY * CZ)
    far_field = far_blocks.transpose(0, 2, 1).reshape(DIRS, 8) * norm_scale
    return (fields_out, far_field)
```

```python
import functools
import math

import jax
import jax.numpy as jnp
from jax import lax
from jax.experimental import pallas as pl
from jax.experimental.pallas import tpu as pltpu
from jax.sharding import PartitionSpec as P

TY = 8
STEPS = 4
TILE_MEAN = 6
SLOTS = 18
SPEED = 0.5
WAVE = 0.35
HALO = jnp.bfloat16
AXES = ("gx", "gy", "gz")


def whole():
    return pl.BlockSpec(memory_space=pltpu.VMEM)


def scalars():
    return pl.BlockSpec(memory_space=pltpu.SMEM)


def pack_depth_kernel(fields_ref, pol_ref, mat_ref, out_ref):
    lane = lax.broadcasted_iota(jnp.int32, (16, 128), 1) // 8

    def packed(plane):
        acc = jnp.zeros((16, 128), jnp.float32)
        for x in range(16):
            acc = jnp.where(lane == x, pltpu.roll(plane(x), (8 * x + 4) % 128, 1), acc)
        return acc.astype(HALO)

    def body(a, carry):
        out_ref[a] = packed(lambda x: fields_ref[a, x])
        out_ref[a + 6] = packed(lambda x: pol_ref[a, x])
        return carry

    lax.fori_loop(0, 6, body, 0)
    out_ref[12] = packed(lambda x: mat_ref[x].astype(jnp.float32))


def join_depth(before, after):
    lane = lax.broadcasted_iota(jnp.int32, (16, 128), 1) % 8
    return jnp.where(lane < 4, before.astype(jnp.float32), after.astype(jnp.float32))


def pack_x_kernel(fields_ref, pol_ref, mat_ref, before_ref, after_ref, low_ref, high_ref):
    def put(a, plane):
        for k in range(4):
            low_ref[a, k] = plane(k).astype(HALO)
            high_ref[a, k] = plane(12 + k).astype(HALO)
        depth = join_depth(before_ref[a], after_ref[a]).astype(HALO)
        low_ref[a, 4] = depth
        high_ref[a, 4] = depth

    def body(a, carry):
        put(a, lambda x: fields_ref[a, x])
        put(a + 6, lambda x: pol_ref[a, x])
        return carry

    lax.fori_loop(0, 6, body, 0)
    put(12, lambda x: mat_ref[x].astype(jnp.float32))


def wide_plane(x, a, plane, before_ref, after_ref, left_ref, right_ref):
    if x < 16:
        return plane(x)
    if x < 20:
        return right_ref[a, x - 16].astype(jnp.float32)
    if x < 24:
        return left_ref[a, x - 20].astype(jnp.float32)
    if x == 24:
        return join_depth(before_ref[a], after_ref[a])
    lane = lax.broadcasted_iota(jnp.int32, (16, 128), 1)
    return jnp.where(
        lane < 32,
        right_ref[a, 4].astype(jnp.float32),
        pltpu.roll(left_ref[a, 4].astype(jnp.float32), 64, 1),
    )


def pack_y_kernel(
    fields_ref, pol_ref, mat_ref, before_ref, after_ref, left_ref, right_ref, low_ref, high_ref
):
    top = lax.broadcasted_iota(jnp.int32, (8, 128), 0) < 4

    def put(a, plane):
        for i in range(13):
            p0, p1 = [
                wide_plane(2 * i + k, a, plane, before_ref, after_ref, left_ref, right_ref)
                for k in range(2)
            ]
            low_ref[a, i] = jnp.where(top, p0[0:8], pltpu.roll(p1[0:8], 4, 0)).astype(HALO)
            high_ref[a, i] = jnp.where(top, pltpu.roll(p1[8:16], 4, 0), p0[8:16]).astype(HALO)

    def body(a, carry):
        put(a, lambda x: fields_ref[a, x])
        put(a + 6, lambda x: pol_ref[a, x])
        return carry

    lax.fori_loop(0, 6, body, 0)
    put(12, lambda x: mat_ref[x].astype(jnp.float32))


def window_kernel(
    extents,
    place_ref,
    count_ref,
    index_ref,
    omega_ref,
    damping_ref,
    strength_ref,
    fields_ref,
    pol_ref,
    mat_ref,
    before_ref,
    after_ref,
    left_ref,
    right_ref,
    down_ref,
    up_ref,
    out_ref,
    cur_ref,
    wide_ref,
    coef_ref,
    phasor_ref,
):
    top = lax.broadcasted_iota(jnp.int32, (8, 128), 0) < 4

    def spread(a, plane, store):
        def rows(i):
            lowest = up_ref[a, i].astype(jnp.float32)
            highest = down_ref[a, i].astype(jnp.float32)
            return (
                jnp.where(top, lowest, highest),
                pltpu.roll(jnp.where(top, highest, lowest), 4, 0),
            )

        depth = []
        tail = rows(12)
        for k in range(2):
            body = wide_plane(24 + k, a, plane, before_ref, after_ref, left_ref, right_ref)
            depth.append(jnp.concatenate([body, tail[k]], axis=0))
        for i in range(12):
            tail = rows(i)
            for k in range(2):
                x = 2 * i + k
                body = wide_plane(x, a, plane, before_ref, after_ref, left_ref, right_ref)
                main = jnp.concatenate([body, tail[k]], axis=0)
                side = pltpu.roll(depth[x // 16], (124 - 8 * x) % 128, 1)
                store(x, jnp.concatenate([main, side], axis=1))

    def store_wide(a):
        def store(x, value):
            wide_ref[a, x] = value

        return store

    def body(a, carry):
        spread(a, lambda x: fields_ref[a, x], store_wide(a))
        spread(a + 6, lambda x: pol_ref[a, x], store_wide(a + 6))
        return carry

    lax.fori_loop(0, 6, body, 0)

    table_a, table_b, table_c = [], [], []
    for m in range(4):
        omega, damp, strong = omega_ref[m], damping_ref[m], strength_ref[m]
        full = jnp.full((8, 256), omega, jnp.float32)
        square = full * full
        half = 0.5 * jnp.full((8, 256), damp, jnp.float32)
        under = 1.0 + half
        table_a.append(((2.0 - square) / under)[0:1])
        table_b.append((-(1.0 - half) / under)[0:1])
        table_c.append((jnp.full((8, 256), strong, jnp.float32) * square / under)[0:1])

    def store_coef(x, value):
        a = jnp.zeros((24, 256), jnp.float32)
        b, c = a, a
        for m in range(4):
            hit = value == float(m + 1)
            a = jnp.where(hit, table_a[m], a)
            b = jnp.where(hit, table_b[m], b)
            c = jnp.where(hit, table_c[m], c)
        coef_ref[0, x] = a
        coef_ref[1, x] = b
        coef_ref[2, x] = c
        coef_ref[3, x] = jnp.where(value > 0.0, 1.0, 0.0)

    spread(12, lambda x: mat_ref[x].astype(jnp.float32), store_coef)

    gx, gy, gz = index_ref[0], index_ref[1], index_ref[2]
    row = lax.broadcasted_iota(jnp.int32, (24, 256), 0)
    row = jnp.where(row < 20, row, row - 24) + gy * 16
    lane = lax.broadcasted_iota(jnp.int32, (24, 256), 1)
    near = (lane < 132) | (lane >= 252)
    lane = jnp.where(lane < 132, lane, lane - 256) + gz * 128
    inside = near & (row >= 0) & (row < extents[1]) & (lane >= 0) & (lane < extents[2])
    inside = jnp.where(inside, SPEED, 0.0).astype(jnp.float32)
    phasor_ref[...] = jnp.zeros_like(phasor_ref)

    def ahead_y(v):
        return pltpu.roll(v, 23, 0)

    def behind_y(v):
        return pltpu.roll(v, 1, 0)

    def ahead_z(v):
        return pltpu.roll(v, 255, 1)

    def behind_z(v):
        return pltpu.roll(v, 1, 1)

    def plane_step(n, x, inner):
        here = jnp.where(x < 0, x + 24, x)
        after = jnp.where(x + 1 < 0, x + 25, x + 1)
        prior = jnp.where(x < 1, x + 23, x - 1)
        place = gx * 16 + x
        speed = inside * jnp.where((place >= 0) & (place < extents[0]), 1.0, 0.0)
        ex, ey, ez = wide_ref[0, here], wide_ref[1, here], wide_ref[2, here]
        ey_next, ez_next = wide_ref[1, after], wide_ref[2, after]
        hx = wide_ref[3, here] - speed * ((ahead_y(ez) - ez) - (ahead_z(ey) - ey))
        hy = wide_ref[4, here] - speed * ((ahead_z(ex) - ex) - (ez_next - ez))
        hz = wide_ref[5, here] - speed * ((ey_next - ey) - (ahead_y(ex) - ex))
        wide_ref[3, here] = hx
        wide_ref[4, here] = hy
        wide_ref[5, here] = hz
        hy_prior, hz_prior = wide_ref[4, prior], wide_ref[5, prior]
        sat = 1.0 / (1.0 + ex * ex + ey * ey + ez * ez)
        a, b, sheet = coef_ref[0, here], coef_ref[1, here], coef_ref[3, here]
        drive = coef_ref[2, here] * sat
        now, old = (6, 9) if n % 2 == 0 else (9, 6)
        curls = (
            (hz - behind_y(hz)) - (hy - behind_z(hy)),
            (hx - behind_z(hx)) - (hz - hz_prior),
            (hy - hy_prior) - (hx - behind_y(hx)),
        )
        fresh = []
        for c, e in enumerate((ex, ey, ez)):
            pol = wide_ref[now + c, here]
            pol_new = a * pol + b * wide_ref[old + c, here] + drive * e
            wide_ref[old + c, here] = pol_new
            value = e + speed * curls[c] - sheet * (pol_new - pol)
            wide_ref[c, here] = value
            fresh.append(value)
        if inner:
            angle_h = WAVE * SPEED * (n + 0.5)
            angle_e = WAVE * SPEED * (n + 1.0)
            hy, hz = hy[0:16, 0:128], hz[0:16, 0:128]
            ey, ez = fresh[1][0:16, 0:128], fresh[2][0:16, 0:128]
            terms = (
                (-math.cos(angle_h), hz),
                (math.cos(angle_h), hy),
                (math.cos(angle_e), ez),
                (-math.cos(angle_e), ey),
                (math.sin(angle_h), hz),
                (-math.sin(angle_h), hy),
                (-math.sin(angle_e), ez),
                (math.sin(angle_e), ey),
            )
            for o, (factor, value) in enumerate(terms):
                phasor_ref[o, x] = phasor_ref[o, x] + factor * value
            if n == STEPS - 1:
                for c in range(3):
                    out_ref[c, x] = fresh[c][0:16, 0:128]
                out_ref[3, x] = hx[0:16, 0:128]
                out_ref[4, x] = hy
                out_ref[5, x] = hz

    for n in range(STEPS):
        for first, last, inner in ((n - 4, 0, False), (0, 16, True), (16, 19 - n, False)):

            def step(x, carry, n=n, inner=inner):
                plane_step(n, x, inner)
                return carry

            lax.fori_loop(first, last, step, 0)

    count = count_ref[0, gz]

    def put_tile(t, carry):
        p = place_ref[0, gz, t]
        live = jnp.where(t < count, 1.0, 0.0)
        rows = pl.ds(pl.multiple_of((p & 1) * 8, 8), 8)
        for o in range(8):
            cur_ref[pl.ds(pl.multiple_of(t * 64 + o * 8, 8), 8), :] = phasor_ref[o, p >> 1, rows, :] * live
        return carry

    lax.fori_loop(0, SLOTS, put_tile, 0)


def kernel_options(mib):
    return pltpu.CompilerParams(vmem_limit_bytes=mib << 20)


def shift(block, axis, by):
    count = lax.axis_size(axis)
    pairs = [(i, i + by) for i in range(count) if 0 <= i + by < count]
    return lax.ppermute(block, axis, pairs)


def window(fields, polarization, material, omega0, damping, strength, count, place, index, sizes):
    own = (fields, polarization, material)
    depth = pl.pallas_call(
        pack_depth_kernel,
        out_shape=jax.ShapeDtypeStruct((13, 16, 128), HALO),
        in_specs=[whole()] * 3,
        out_specs=whole(),
        compiler_params=kernel_options(6),
        name="pack_depth",
    )(*own)
    before, after = shift(depth, "gz", 1), shift(depth, "gz", -1)
    low, high = pl.pallas_call(
        pack_x_kernel,
        out_shape=(jax.ShapeDtypeStruct((13, 5, 16, 128), HALO),) * 2,
        in_specs=[whole()] * 5,
        out_specs=(whole(),) * 2,
        compiler_params=kernel_options(6),
        name="pack_x",
    )(*own, before, after)
    left, right = shift(high, "gx", 1), shift(low, "gx", -1)
    low, high = pl.pallas_call(
        pack_y_kernel,
        out_shape=(jax.ShapeDtypeStruct((13, 13, 8, 128), HALO),) * 2,
        in_specs=[whole()] * 7,
        out_specs=(whole(),) * 2,
        compiler_params=kernel_options(6),
        name="pack_y",
    )(*own, before, after, left, right)
    down, up = shift(high, "gy", 1), shift(low, "gy", -1)
    return pl.pallas_call(
        functools.partial(window_kernel, sizes),
        out_shape=(
            jax.ShapeDtypeStruct((6, 16, 16, 128), jnp.float32),
            jax.ShapeDtypeStruct((SLOTS * 64, 128), jnp.float32),
        ),
        in_specs=[scalars()] * 6 + [whole()] * 9,
        out_specs=(whole(),) * 2,
        scratch_shapes=[
            pltpu.VMEM((12, 24, 24, 256), jnp.float32),
            pltpu.VMEM((4, 24, 24, 256), jnp.float32),
            pltpu.VMEM((8, 16, 16, 128), jnp.float32),
        ],
        compiler_params=kernel_options(24),
        name="window",
    )(place, count, index, omega0, damping, strength, *own, before, after, left, right, down, up)


TWO_PI = 2.0 * math.pi
TURN = 0.35 / TWO_PI
PAIRS = 4 * SLOTS


def sin_quarter(y):
    z = y * y
    c = [TWO_PI ** n * s / math.factorial(n) for n, s in ((1, 1), (3, -1), (5, 1), (7, -1), (9, 1), (11, -1))]
    acc = jnp.full_like(z, c[5])
    for k in (4, 3, 2, 1, 0):
        acc = acc * z + c[k]
    return acc * y


def cos_sin(turns):
    r = turns - jnp.floor(turns + 0.5)
    a = jnp.abs(r)
    cos = sin_quarter(0.25 - a)
    sin = sin_quarter(0.25 - jnp.abs(a - 0.25))
    return cos, jnp.where(r < 0, -sin, sin)


def dirs_kernel(angles_ref, order_ref, u_ref):
    idx = order_ref[...]
    hi = idx >> 7
    lo = idx & 127

    def body(h, acc):
        polar, azim = acc
        pick = hi == h
        row_p = jnp.broadcast_to(angles_ref[0, pl.ds(h, 1), :], lo.shape)
        row_a = jnp.broadcast_to(angles_ref[1, pl.ds(h, 1), :], lo.shape)
        polar = jnp.where(pick, jnp.take_along_axis(row_p, lo, axis=1), polar)
        azim = jnp.where(pick, jnp.take_along_axis(row_a, lo, axis=1), azim)
        return polar, azim

    zero = jnp.zeros(idx.shape, jnp.float32)
    polar, azim = lax.fori_loop(0, 64, body, (zero, zero))
    cos_p, sin_p = cos_sin(polar * (1.0 / TWO_PI))
    cos_a, sin_a = cos_sin(azim * (1.0 / TWO_PI))
    u_ref[0] = sin_p * cos_a
    u_ref[1] = sin_p * sin_a
    u_ref[2] = cos_p


def directions(dir_angles, dir_order):
    order = dir_order.reshape(256, 32).T.reshape(64, 128)
    return pl.pallas_call(
        dirs_kernel,
        out_shape=jax.ShapeDtypeStruct((3, 64, 128), jnp.float32),
        in_specs=[pl.BlockSpec(memory_space=pltpu.VMEM)] * 2,
        out_specs=pl.BlockSpec(memory_space=pltpu.VMEM),
        cost_estimate=pl.CostEstimate(flops=3000000, bytes_accessed=300000, transcendentals=0),
        compiler_params=kernel_options(12),
        name="dirs",
    )(dir_angles.reshape(2, 64, 128), order)


def tables_kernel(place_ref, index_ref, u_ref, table_ref, weight_ref, pos_ref):
    @pl.when(pl.program_id(0) == 0)
    def _():
        gx, gy, gz = index_ref[0], index_ref[1], index_ref[2]
        pos_ref[...] = jnp.zeros_like(pos_ref)
        for t in range(SLOTS):
            p = place_ref[0, gz, t]
            for axis, start in enumerate((gx * 16 + (p >> 1), gy * 16 + (p & 1) * 8, gz * 128)):
                pos_ref[axis, t : t + 1, :] = jnp.full((1, 256), start.astype(jnp.float32))

    j2 = pl.multiple_of(pl.program_id(0) * 2, 2)

    def row(axis):
        return jnp.concatenate(
            [u_ref[axis, pl.ds(j2, 1), :], u_ref[axis, pl.ds(j2 + 1, 1), :]], axis=1
        ) * TURN

    ux, uy, uz = row(0), row(1), row(2)
    eight = lax.broadcasted_iota(jnp.int32, (8, 256), 0).astype(jnp.float32)
    sixteen = lax.broadcasted_iota(jnp.int32, (16, 256), 0).astype(jnp.float32) * 8.0
    low_c, low_s = cos_sin(uz * eight)
    high_c, high_s = cos_sin(uz * sixteen)
    row_c, row_s = cos_sin(uy * eight)
    one_c, one_s = row_c[1:2], row_s[1:2]
    for pair in range(8):
        rows = ([], [], [], [])
        for half in range(2):
            a = 2 * pair + half
            hc, hs = high_c[a : a + 1], high_s[a : a + 1]
            c = hc * low_c - hs * low_s
            s = hs * low_c + hc * low_s
            rows[0].append(c)
            rows[1].append(c * one_c - s * one_s)
            rows[2].append(s)
            rows[3].append(s * one_c + c * one_s)
        for part in range(4):
            table_ref[0, part * 128 + 16 * pair : part * 128 + 16 * pair + 16, :] = jnp.concatenate(
                rows[part], axis=0
            ).astype(jnp.bfloat16)
    phase = pos_ref[0] * ux + pos_ref[1] * uy + pos_ref[2] * uz
    tile_c, tile_s = cos_sin(phase)
    for g in range(4):
        gc, gs = row_c[2 * g : 2 * g + 1], row_s[2 * g : 2 * g + 1]
        weight_ref[0, 0, 24 * g : 24 * g + 24, :] = tile_c * gc - tile_s * gs
        weight_ref[0, 1, 24 * g : 24 * g + 24, :] = tile_s * gc + tile_c * gs


def tables(u, place, index):
    return pl.pallas_call(
        tables_kernel,
        grid=(32,),
        out_shape=(
            jax.ShapeDtypeStruct((32, 512, 256), jnp.bfloat16),
            jax.ShapeDtypeStruct((32, 2, 96, 256), jnp.float32),
        ),
        in_specs=[
            scalars(),
            scalars(),
            pl.BlockSpec((3, 64, 128), lambda j: (0, 0, 0)),
        ],
        out_specs=(
            pl.BlockSpec((1, 512, 256), lambda j: (j, 0, 0)),
            pl.BlockSpec((1, 2, 96, 256), lambda j: (j, 0, 0, 0)),
        ),
        scratch_shapes=[pltpu.VMEM((3, 24, 256), jnp.float32)],
        cost_estimate=pl.CostEstimate(flops=60000000, bytes_accessed=14000000, transcendentals=0),
        compiler_params=kernel_options(12),
        name="tables",
    )(place, index, u)


def far_kernel(scale, cur_ref, table_ref, weight_ref, out_ref, lhs_ref, acc_ref):
    j = pl.program_id(0)

    @pl.when(j == 0)
    def _():
        sign = jnp.where(lax.broadcasted_iota(jnp.int32, (SLOTS * 8, 128), 0) % 8 < 4, -1.0, 1.0)
        for ty in range(8):
            g, half = ty // 2, ty % 2
            plain = cur_ref[pl.ds(ty, SLOTS * 8, stride=8), :]
            swapped = pltpu.roll(plain.reshape(SLOTS, 8, 128), 4, 1).reshape(SLOTS * 8, 128) * sign
            rows = slice(g * SLOTS * 8, (g + 1) * SLOTS * 8)
            lhs_ref[rows, half * 128 : half * 128 + 128] = plain.astype(jnp.bfloat16)
            lhs_ref[rows, 256 + half * 128 : 384 + half * 128] = swapped.astype(jnp.bfloat16)

    prod = jnp.dot(lhs_ref[...], table_ref[0], preferred_element_type=jnp.float32)
    first = jnp.zeros((8, 256), jnp.float32)
    second = jnp.zeros((8, 256), jnp.float32)
    for g in range(4):
        for t in range(SLOTS):
            row = 8 * (g * SLOTS + t)
            piece = prod[row : row + 8]
            first = first + piece * weight_ref[0, 0, pl.ds(24 * g + t, 8, stride=0), :]
            second = second + piece * weight_ref[0, 1, pl.ds(24 * g + t, 8, stride=0), :]
    sign = jnp.where(lax.broadcasted_iota(jnp.int32, (8, 256), 0) < 4, -scale, scale)
    acc_ref[pl.ds(pl.multiple_of(j * 8, 8), 8), :] = first * scale + pltpu.roll(second, 4, 0) * sign

    @pl.when(j == pl.num_programs(0) - 1)
    def _():
        out_ref[...] = acc_ref[...].T.astype(out_ref.dtype)


def far_products(currents, table, weight, scale, dtype):
    return pl.pallas_call(
        functools.partial(far_kernel, scale),
        grid=(32,),
        out_shape=jax.ShapeDtypeStruct((256, 256), dtype),
        in_specs=[
            pl.BlockSpec((SLOTS * 64, 128), lambda j: (0, 0)),
            pl.BlockSpec((1, 512, 256), lambda j: (j, 0, 0)),
            pl.BlockSpec((1, 2, 96, 256), lambda j: (j, 0, 0, 0)),
        ],
        out_specs=pl.BlockSpec((256, 256), lambda j: (0, 0)),
        scratch_shapes=[
            pltpu.VMEM((4 * SLOTS * 8, 512), jnp.bfloat16),
            pltpu.VMEM((256, 256), jnp.float32),
        ],
        cost_estimate=pl.CostEstimate(flops=5000000000, bytes_accessed=15000000, transcendentals=0),
        compiler_params=kernel_options(12),
        name="far",
    )(currents, table, weight)


def sum_kernel(in_ref, out_ref):
    total = jnp.sum(in_ref[...].astype(jnp.float32), axis=0, keepdims=True)
    spread = jnp.where(
        lax.broadcasted_iota(jnp.int32, (32, 256), 1) // 8 == lax.broadcasted_iota(jnp.int32, (32, 256), 0),
        jnp.broadcast_to(total, (32, 256)),
        0.0,
    )
    row = lax.broadcasted_iota(jnp.int32, (256, 8), 0) % 8
    col = lax.broadcasted_iota(jnp.int32, (256, 8), 1)
    pick = jnp.where((row % 4) * 2 + row // 4 == col, 1.0, 0.0)
    out_ref[...] = jnp.dot(
        spread, pick, preferred_element_type=jnp.float32, precision=lax.Precision.HIGHEST
    )


def sum_sources(received):
    return pl.pallas_call(
        sum_kernel,
        out_shape=jax.ShapeDtypeStruct((32, 8), jnp.float32),
        in_specs=[pl.BlockSpec(memory_space=pltpu.VMEM)],
        out_specs=pl.BlockSpec(memory_space=pltpu.VMEM),
        compiler_params=kernel_options(12),
        name="sum_sources",
    )(received)


def shards(
    fields,
    polarization,
    material,
    omega0,
    damping,
    strength,
    tile_count,
    tile_place,
    dir_angles,
    dir_order,
):
    sizes = tuple(lax.axis_size(axis) * n for axis, n in zip(AXES, fields.shape[1:]))
    index = jnp.stack([lax.axis_index(axis) for axis in AXES]).astype(jnp.int32)
    table, weight = tables(directions(dir_angles, dir_order), tile_place, index)
    fields_out, currents = window(
        fields,
        polarization,
        material,
        omega0,
        damping,
        strength,
        tile_count,
        tile_place,
        index,
        sizes,
    )
    tile_total = math.prod(lax.axis_size(axis) for axis in AXES) * TILE_MEAN
    scale = 1.0 / math.sqrt(tile_total * TY * fields.shape[3])
    partial = far_products(currents, table, weight, scale, jnp.bfloat16)
    received = lax.all_to_all(partial, AXES, 0, 0, tiled=True)
    return fields_out, sum_sources(received)


def solution(mesh):
    return jax.shard_map(
        shards,
        mesh=mesh,
        in_specs=(
            P(None, *AXES),
            P(None, *AXES),
            P(*AXES),
            P(),
            P(),
            P(),
            P(("gx", "gy"), None),
            P(("gx", "gy"), None, None),
            P(),
            P(),
        ),
        out_specs=(P(None, *AXES), P(AXES, None)),
        check_vma=False,
    )
```

```python
import functools
import math

import jax
import jax.numpy as jnp
from jax import lax
from jax.experimental import pallas as pl
from jax.experimental.pallas import tpu as pltpu
from jax.sharding import PartitionSpec as P

TY = 8
STEPS = 4
TILE_MEAN = 6
SLOTS = 18
SPEED = 0.5
WAVE = 0.35
HALO = jnp.bfloat16
BLOCK = 8
PER_STEP = 4
AXES = ("gx", "gy", "gz")


def whole():
    return pl.BlockSpec(memory_space=pltpu.VMEM)


def scalars():
    return pl.BlockSpec(memory_space=pltpu.SMEM)


def pack_depth_kernel(fields_ref, pol_ref, mat_ref, out_ref, buf_ref, raw_ref, sems):
    lane = lax.broadcasted_iota(jnp.int32, (16, 128), 1) // 8
    copies = [pltpu.make_async_copy(fields_ref.at[a], buf_ref.at[a], sems.at[a]) for a in range(6)]
    copies += [
        pltpu.make_async_copy(pol_ref.at[a], buf_ref.at[a + 6], sems.at[a + 6]) for a in range(6)
    ]
    copies.append(pltpu.make_async_copy(mat_ref, raw_ref, sems.at[12]))
    for copy in copies:
        copy.start()
    for a, copy in enumerate(copies):
        copy.wait()
        acc = jnp.zeros((16, 128), jnp.float32)
        for x in range(16):
            plane = raw_ref[x].astype(jnp.float32) if a == 12 else buf_ref[a, x]
            acc = jnp.where(lane == x, pltpu.roll(plane, (8 * x + 4) % 128, 1), acc)
        out_ref[a] = acc.astype(HALO)


def stage_kernel(fields_ref, pol_ref, mat_ref, own_ref):
    own_ref[0:6] = fields_ref[...]
    own_ref[6:12] = pol_ref[...]
    own_ref[12] = mat_ref[...].astype(jnp.float32)


def join_depth(before, after):
    lane = lax.broadcasted_iota(jnp.int32, (16, 128), 1) % 8
    return jnp.where(lane < 4, before.astype(jnp.float32), after.astype(jnp.float32))


def pack_x_kernel(own_ref, before_ref, after_ref, low_ref, high_ref):
    def body(a, carry):
        for k in range(3):
            low_ref[a * 3 + k] = own_ref[a, k].astype(HALO)
            high_ref[a * 3 + k] = own_ref[a, 13 + k].astype(HALO)
        return carry

    lax.fori_loop(0, 13, body, 0)
    for k, a in enumerate((1, 2)):
        low_ref[39 + k] = own_ref[a, 3].astype(HALO)
    for k, a in enumerate((0, 1, 2, 4, 5)):
        high_ref[39 + k] = own_ref[a, 12].astype(HALO)
    group = lax.broadcasted_iota(jnp.int32, (16, 128), 1) // 32
    for q in range(4):
        low = jnp.zeros((16, 128), jnp.float32)
        high = low
        for r in range(min(4, 13 - 4 * q)):
            depth = join_depth(before_ref[4 * q + r], after_ref[4 * q + r])
            low = jnp.where(group == r, pltpu.roll(depth, 32 * r, 1) if r else depth, low)
            high = jnp.where(group == r, pltpu.roll(depth, 32 * r + 32, 1) if r < 3 else depth, high)
        low_ref[41 + q] = low.astype(HALO)
        high_ref[44 + q] = high.astype(HALO)


def wide_plane(x, a, own_ref, before_ref, after_ref, left_ref, right_ref):
    if x < 16:
        return own_ref[a, x]
    if x < 19:
        return right_ref[a * 3 + x - 16].astype(jnp.float32)
    if x == 19:
        return right_ref[39 + jnp.clip(a - 1, 0, 1)].astype(jnp.float32)
    if x == 20:
        return left_ref[39 + jnp.minimum(jnp.where(a < 3, a, a - 1), 4)].astype(jnp.float32)
    if x < 24:
        return left_ref[a * 3 + x - 21].astype(jnp.float32)
    if x == 24:
        return join_depth(before_ref[a], after_ref[a])
    lane = lax.broadcasted_iota(jnp.int32, (16, 128), 1)
    turn = 32 * (a % 4)
    return jnp.where(
        lane < 32,
        pltpu.roll(right_ref[41 + a // 4].astype(jnp.float32), (128 - turn) % 128, 1),
        pltpu.roll(left_ref[44 + a // 4].astype(jnp.float32), (160 - turn) % 128, 1),
    )


def pack_y_kernel(
    own_ref, before_ref, after_ref, left_ref, right_ref, u_ref, low_ref, high_ref
):
    top = lax.broadcasted_iota(jnp.int32, (8, 128), 0) < 4

    def body(a, carry):
        for i in range(13):
            p0, p1 = [
                wide_plane(2 * i + k, a, own_ref, before_ref, after_ref, left_ref, right_ref)
                for k in range(2)
            ]
            low_ref[a, i] = jnp.where(top, p0[0:8], pltpu.roll(p1[0:8], 4, 0)).astype(HALO)
            high_ref[a, i] = jnp.where(top, pltpu.roll(p1[8:16], 4, 0), p0[8:16]).astype(HALO)
        return carry

    lax.fori_loop(0, 13, body, 0)


def side_lanes(depth, x):
    return pltpu.roll(depth[x // 16], (124 - 8 * x) % 128, 1)


def coefficients(medium_ref, value):
    shape = value.shape
    a = jnp.zeros(shape, jnp.float32)
    b, c = a, a
    for m in range(4):
        omega = jnp.full((8, 128), medium_ref[m], jnp.float32)
        half = 0.5 * jnp.full((8, 128), medium_ref[4 + m], jnp.float32)
        strong = jnp.full((8, 128), medium_ref[8 + m], jnp.float32)
        square = omega * omega
        under = 1.0 + half
        hit = value == float(m + 1)
        wide = (lambda v: jnp.broadcast_to(jnp.concatenate([v[0:1]] * 2, axis=1), shape))
        a = jnp.where(hit, wide((2.0 - square) / under), a)
        b = jnp.where(hit, wide(-(1.0 - half) / under), b)
        c = jnp.where(hit, wide(strong * square / under), c)
    return a, b, c, jnp.where(value > 0.0, 1.0, 0.0)


def lay_kernel(
    medium_ref, own_ref, before_ref, after_ref, left_ref, right_ref, low_ref, wide_ref, coef_ref
):
    def spread(a, store):
        depth = [
            wide_plane(24 + k, a, own_ref, before_ref, after_ref, left_ref, right_ref)
            for k in range(2)
        ]
        for x in range(24):
            main = wide_plane(x, a, own_ref, before_ref, after_ref, left_ref, right_ref)
            store(x, jnp.concatenate([main, side_lanes(depth, x)], axis=1))

    def body(a, carry):
        def store(x, value):
            wide_ref[a, x] = value

        spread(a, store)
        return carry

    lax.fori_loop(0, 12, body, 0)

    def store_coef(x, value):
        for k, coef in enumerate(coefficients(medium_ref, value)):
            coef_ref[k, x] = coef

    spread(jnp.int32(12), store_coef)


def window_kernel(
    extents,
    ints_ref,
    medium_ref,
    laid_ref,
    laid_coef_ref,
    down_ref,
    up_ref,
    out_ref,
    cur_ref,
    wide_ref,
    tail_ref,
    tail_coef_ref,
    phasor_ref,
):
    top = lax.broadcasted_iota(jnp.int32, (8, 128), 0) < 4

    def spread(a, store):
        def rows(i):
            lowest = up_ref[a, i].astype(jnp.float32)
            highest = down_ref[a, i].astype(jnp.float32)
            return (
                jnp.where(top, lowest, highest),
                pltpu.roll(jnp.where(top, highest, lowest), 4, 0),
            )

        depth = rows(12)
        for i in range(12):
            tail = rows(i)
            for k in range(2):
                x = 2 * i + k
                store(x, jnp.concatenate([tail[k], side_lanes(depth, x)], axis=1))

    def body(a, carry):
        def store(x, value):
            tail_ref[a, x] = value

        spread(a, store)
        return carry

    lax.fori_loop(0, 12, body, 0)

    def store_coef(x, value):
        for k, coef in enumerate(coefficients(medium_ref, value)):
            tail_coef_ref[k, x] = coef

    spread(12, store_coef)

    def first_value(k, x):
        return jnp.concatenate([laid_ref[k, x], tail_ref[k, x]], axis=0)

    def coefficient(k, x):
        return jnp.concatenate([laid_coef_ref[k, x], tail_coef_ref[k, x]], axis=0)

    gx, gy, gz = ints_ref[76], ints_ref[77], ints_ref[78]
    row = lax.broadcasted_iota(jnp.int32, (24, 256), 0)
    row = jnp.where(row < 20, row, row - 24) + gy * 16
    lane = lax.broadcasted_iota(jnp.int32, (24, 256), 1)
    near = (lane < 132) | (lane >= 252)
    lane = jnp.where(lane < 132, lane, lane - 256) + gz * 128
    inside = near & (row >= 0) & (row < extents[1]) & (lane >= 0) & (lane < extents[2])
    inside = jnp.where(inside, SPEED, 0.0).astype(jnp.float32)

    def ahead_y(v):
        return pltpu.roll(v, 23, 0)

    def behind_y(v):
        return pltpu.roll(v, 1, 0)

    def ahead_z(v):
        return pltpu.roll(v, 255, 1)

    def behind_z(v):
        return pltpu.roll(v, 1, 1)

    def wrap(x):
        return jnp.where(x < 0, x + 24, x) if not isinstance(x, int) else x % 24

    def magnetic_step(n, x):
        here, after = wrap(x), wrap(x + 1)
        place = gx * 16 + x
        speed = inside * jnp.where((place >= 0) & (place < extents[0]), 1.0, 0.0)
        get = first_value if n == 0 else (lambda k, at: wide_ref[k, at])
        ex, ey, ez = get(0, here), get(1, here), get(2, here)
        ey_next, ez_next = get(1, after), get(2, after)
        hx = get(3, here) - speed * ((ahead_y(ez) - ez) - (ahead_z(ey) - ey))
        hy = get(4, here) - speed * ((ahead_z(ex) - ex) - (ez_next - ez))
        hz = get(5, here) - speed * ((ey_next - ey) - (ahead_y(ex) - ex))
        wide_ref[3, here] = hx
        wide_ref[4, here] = hy
        wide_ref[5, here] = hz
        return speed, hx, hy, hz

    def electric_step(n, x, inner, speed, hx, hy, hz):
        here, prior = wrap(x), wrap(x - 1)
        last = n == STEPS - 1

        def cut(v):
            return v[0:16, 0:128] if last else v

        now, old = (6, 9) if n % 2 == 0 else (9, 6)

        def get(k, at, fresh=True):
            if fresh and (n == 0 or (n == 1 and k >= 6 and k < 9)):
                return first_value(k, at)
            return wide_ref[k, at, 0:16, 0:128] if last else wide_ref[k, at]

        def get_coef(k):
            return laid_coef_ref[k, here, 0:16, 0:128] if last else coefficient(k, here)

        def put(k, value):
            if last:
                wide_ref[k, here, 0:16, 0:128] = value
            else:
                wide_ref[k, here] = value

        ex, ey, ez = get(0, here), get(1, here), get(2, here)
        hy_prior, hz_prior = get(4, prior, False), get(5, prior, False)
        sat = 1.0 / (1.0 + ex * ex + ey * ey + ez * ez)
        a, b, sheet = get_coef(0), get_coef(1), get_coef(3)
        drive = get_coef(2) * sat
        hxc, hyc, hzc = cut(hx), cut(hy), cut(hz)
        curls = (
            (hzc - cut(behind_y(hz))) - (hyc - cut(behind_z(hy))),
            (hxc - cut(behind_z(hx))) - (hzc - hz_prior),
            (hyc - hy_prior) - (hxc - cut(behind_y(hx))),
        )
        rate = cut(speed)
        fresh = []
        for c, e in enumerate((ex, ey, ez)):
            pol = get(now + c, here)
            pol_new = a * pol + b * get(old + c, here) + drive * e
            value = e + rate * curls[c] - sheet * (pol_new - pol)
            if last:
                out_ref[c, x] = value
            else:
                put(old + c, pol_new)
                put(c, value)
            fresh.append(value)
        if inner:
            angle_h = WAVE * SPEED * (n + 0.5)
            angle_e = WAVE * SPEED * (n + 1.0)
            hxc, hyc, hzc = hx[0:16, 0:128], hy[0:16, 0:128], hz[0:16, 0:128]
            ey, ez = fresh[1][0:16, 0:128], fresh[2][0:16, 0:128]
            terms = (
                (-math.cos(angle_h), hzc),
                (math.cos(angle_h), hyc),
                (math.cos(angle_e), ez),
                (-math.cos(angle_e), ey),
                (math.sin(angle_h), hzc),
                (-math.sin(angle_h), hyc),
                (-math.sin(angle_e), ez),
                (math.sin(angle_e), ey),
            )
            for o, (factor, value) in enumerate(terms):
                phasor_ref[o, x] = factor * value if n == 0 else phasor_ref[o, x] + factor * value
            if last:
                out_ref[3, x] = hxc
                out_ref[4, x] = hyc
                out_ref[5, x] = hzc

    def block_step(n, first, count, inner):
        states = [magnetic_step(n, first + k) for k in range(count)]
        if n == STEPS - 1 and not inner:
            return
        for k, state in enumerate(states):
            electric_step(n, first + k, inner, *state)

    for k in (4, 5):
        wide_ref[k, 19] = jnp.zeros((24, 256), jnp.float32)

    for n in range(STEPS):
        block_step(n, n - 4, 4 - n, False)

        def step(i, carry, n=n):
            block_step(n, i * BLOCK, BLOCK, True)
            return carry

        lax.fori_loop(0, 16 // BLOCK, step, 0)
        if n < STEPS - 1:
            block_step(n, 16, 3 - n, False)

    count = ints_ref[72 + gz]

    def put_tile(t, carry):
        p = ints_ref[gz * SLOTS + t]
        live = jnp.where(t < count, 1.0, 0.0)
        rows = pl.ds(pl.multiple_of((p & 1) * 8, 8), 8)
        for o in range(8):
            cur_ref[pl.ds(pl.multiple_of(t * 64 + o * 8, 8), 8), :] = phasor_ref[o, p >> 1, rows, :] * live
        return carry

    lax.fori_loop(0, SLOTS, put_tile, 0)


def kernel_options(mib):
    return pltpu.CompilerParams(vmem_limit_bytes=mib << 20)


def shift(block, axis, by):
    count = lax.axis_size(axis)
    pairs = [(i, i + by) for i in range(count) if 0 <= i + by < count]
    return lax.ppermute(block, axis, pairs)


def window(fields, polarization, material, medium, ints, sizes, dir_angles, dir_order):
    anywhere = pl.BlockSpec(memory_space=pl.ANY)
    depth = pl.pallas_call(
        pack_depth_kernel,
        out_shape=jax.ShapeDtypeStruct((13, 16, 128), HALO),
        in_specs=[pl.BlockSpec(memory_space=pltpu.HBM)] * 3,
        out_specs=whole(),
        scratch_shapes=[
            pltpu.VMEM((12, 16, 16, 128), jnp.float32),
            pltpu.VMEM((16, 16, 128), jnp.int32),
            pltpu.SemaphoreType.DMA((13,)),
        ],
        compiler_params=pltpu.CompilerParams(vmem_limit_bytes=65000 << 10),
        name="pack_depth",
    )(fields, polarization, material)
    later, _ = lax.optimization_barrier(((fields, polarization, material), depth))
    own = pl.pallas_call(
        stage_kernel,
        out_shape=jax.ShapeDtypeStruct((13, 16, 16, 128), jnp.float32),
        in_specs=[whole()] * 3,
        out_specs=whole(),
        compiler_params=kernel_options(6),
        name="stage",
    )(*later)
    before, after = shift(depth, "gz", 1), shift(depth, "gz", -1)
    low, high = pl.pallas_call(
        pack_x_kernel,
        out_shape=(
            jax.ShapeDtypeStruct((45, 16, 128), HALO),
            jax.ShapeDtypeStruct((48, 16, 128), HALO),
        ),
        in_specs=[whole()] * 3,
        out_specs=(whole(),) * 2,
        compiler_params=kernel_options(6),
        name="pack_x",
    )(own, before, after)
    left, right = shift(high, "gx", 1), shift(low, "gx", -1)
    u = directions(dir_angles, dir_order, low)
    table, weight = tables(u, ints, low)
    low, high = pl.pallas_call(
        pack_y_kernel,
        out_shape=(jax.ShapeDtypeStruct((13, 13, 8, 128), HALO),) * 2,
        in_specs=[whole()] * 5 + [anywhere],
        out_specs=(whole(),) * 2,
        compiler_params=kernel_options(6),
        name="pack_y",
    )(own, before, after, left, right, weight)
    laid, laid_coef = pl.pallas_call(
        lay_kernel,
        out_shape=(
            jax.ShapeDtypeStruct((12, 24, 16, 256), jnp.float32),
            jax.ShapeDtypeStruct((4, 24, 16, 256), jnp.float32),
        ),
        in_specs=[scalars()] + [whole()] * 5 + [anywhere],
        out_specs=(whole(),) * 2,
        compiler_params=kernel_options(10),
        cost_estimate=pl.CostEstimate(flops=8000000, bytes_accessed=9000000, transcendentals=0),
        name="lay",
    )(medium, own, before, after, left, right, low)
    down, up = shift(high, "gy", 1), shift(low, "gy", -1)
    fields_out, currents = pl.pallas_call(
        functools.partial(window_kernel, sizes),
        out_shape=(
            jax.ShapeDtypeStruct((6, 16, 16, 128), jnp.float32),
            jax.ShapeDtypeStruct((SLOTS * 64, 128), jnp.float32),
        ),
        in_specs=[scalars()] * 2 + [whole()] * 4,
        out_specs=(whole(),) * 2,
        scratch_shapes=[
            pltpu.VMEM((12, 24, 24, 256), jnp.float32),
            pltpu.VMEM((12, 24, 8, 256), jnp.float32),
            pltpu.VMEM((4, 24, 8, 256), jnp.float32),
            pltpu.VMEM((8, 16, 16, 128), jnp.float32),
        ],
        compiler_params=kernel_options(24),
        name="window",
    )(ints, medium, laid, laid_coef, down, up)
    return fields_out, currents, table, weight


TWO_PI = 2.0 * math.pi
TURN = 0.35 / TWO_PI
PAIRS = 4 * SLOTS


def sin_quarter(y):
    z = y * y
    c = [TWO_PI ** n * s / math.factorial(n) for n, s in ((1, 1), (3, -1), (5, 1), (7, -1), (9, 1), (11, -1))]
    acc = jnp.full_like(z, c[5])
    for k in (4, 3, 2, 1, 0):
        acc = acc * z + c[k]
    return acc * y


def cos_sin(turns):
    r = turns - jnp.floor(turns + 0.5)
    a = jnp.abs(r)
    cos = sin_quarter(0.25 - a)
    sin = sin_quarter(0.25 - jnp.abs(a - 0.25))
    return cos, jnp.where(r < 0, -sin, sin)


def dirs_kernel(angles_ref, order_ref, low_ref, u_ref):
    idx = order_ref[...]
    hi = idx >> 7
    lo = idx & 127

    def body(h, acc):
        polar, azim = acc
        pick = hi == h
        row_p = jnp.broadcast_to(angles_ref[0, pl.ds(h, 1), :], lo.shape)
        row_a = jnp.broadcast_to(angles_ref[1, pl.ds(h, 1), :], lo.shape)
        polar = jnp.where(pick, jnp.take_along_axis(row_p, lo, axis=1), polar)
        azim = jnp.where(pick, jnp.take_along_axis(row_a, lo, axis=1), azim)
        return polar, azim

    zero = jnp.zeros(idx.shape, jnp.float32)
    polar, azim = lax.fori_loop(0, 64, body, (zero, zero), unroll=4)
    cos_p, sin_p = cos_sin(polar * (1.0 / TWO_PI))
    cos_a, sin_a = cos_sin(azim * (1.0 / TWO_PI))
    u_ref[0] = sin_p * cos_a
    u_ref[1] = sin_p * sin_a
    u_ref[2] = cos_p


def directions(dir_angles, dir_order, low):
    order = dir_order.reshape(256, 32).T.reshape(64, 128)
    return pl.pallas_call(
        dirs_kernel,
        out_shape=jax.ShapeDtypeStruct((3, 64, 128), jnp.float32),
        in_specs=[whole(), whole(), pl.BlockSpec(memory_space=pl.ANY)],
        out_specs=whole(),
        cost_estimate=pl.CostEstimate(flops=3000000, bytes_accessed=300000, transcendentals=0),
        compiler_params=kernel_options(12),
        name="dirs",
    )(dir_angles.reshape(2, 64, 128), order, low)


def tables_kernel(ints_ref, low_ref, u_ref, table_ref, weight_ref, pos_ref):
    @pl.when(pl.program_id(0) == 0)
    def _():
        gx, gy, gz = ints_ref[76], ints_ref[77], ints_ref[78]
        pos_ref[...] = jnp.zeros_like(pos_ref)
        for t in range(SLOTS):
            p = ints_ref[gz * SLOTS + t]
            for axis, start in enumerate((gx * 16 + (p >> 1), gy * 16 + (p & 1) * 8, gz * 128)):
                pos_ref[axis, t : t + 1, :] = jnp.full((1, 256), start.astype(jnp.float32))

    j2 = pl.multiple_of(pl.program_id(0) * 2, 2)

    def row(axis):
        return jnp.concatenate(
            [u_ref[axis, pl.ds(j2, 1), :], u_ref[axis, pl.ds(j2 + 1, 1), :]], axis=1
        ) * TURN

    ux, uy, uz = row(0), row(1), row(2)
    eight = lax.broadcasted_iota(jnp.int32, (8, 256), 0).astype(jnp.float32)
    sixteen = lax.broadcasted_iota(jnp.int32, (16, 256), 0).astype(jnp.float32) * 8.0
    low_c, low_s = cos_sin(uz * eight)
    high_c, high_s = cos_sin(uz * sixteen)
    row_c, row_s = cos_sin(uy * eight)
    one_c, one_s = row_c[1:2], row_s[1:2]
    for pair in range(8):
        rows = ([], [], [], [])
        for half in range(2):
            a = 2 * pair + half
            hc, hs = high_c[a : a + 1], high_s[a : a + 1]
            c = hc * low_c - hs * low_s
            s = hs * low_c + hc * low_s
            rows[0].append(c)
            rows[1].append(c * one_c - s * one_s)
            rows[2].append(s)
            rows[3].append(s * one_c + c * one_s)
        for part in range(4):
            table_ref[0, part * 128 + 16 * pair : part * 128 + 16 * pair + 16, :] = jnp.concatenate(
                rows[part], axis=0
            ).astype(jnp.bfloat16)
    phase = pos_ref[0] * ux + pos_ref[1] * uy + pos_ref[2] * uz
    tile_c, tile_s = cos_sin(phase)
    for g in range(4):
        gc, gs = row_c[2 * g : 2 * g + 1], row_s[2 * g : 2 * g + 1]
        weight_ref[0, 0, 24 * g : 24 * g + 24, :] = tile_c * gc - tile_s * gs
        weight_ref[0, 1, 24 * g : 24 * g + 24, :] = tile_s * gc + tile_c * gs


def tables(u, ints, low):
    return pl.pallas_call(
        tables_kernel,
        grid=(32,),
        out_shape=(
            jax.ShapeDtypeStruct((32, 512, 256), jnp.bfloat16),
            jax.ShapeDtypeStruct((32, 2, 96, 256), jnp.float32),
        ),
        in_specs=[
            scalars(),
            pl.BlockSpec(memory_space=pl.ANY),
            pl.BlockSpec((3, 64, 128), lambda j: (0, 0, 0)),
        ],
        out_specs=(
            pl.BlockSpec((1, 512, 256), lambda j: (j, 0, 0)),
            pl.BlockSpec((1, 2, 96, 256), lambda j: (j, 0, 0, 0)),
        ),
        scratch_shapes=[pltpu.VMEM((3, 24, 256), jnp.float32)],
        cost_estimate=pl.CostEstimate(flops=60000000, bytes_accessed=14000000, transcendentals=0),
        compiler_params=kernel_options(12),
        name="tables",
    )(ints, low, u)


def far_kernel(scale, cur_ref, table_ref, weight_ref, out_ref, lhs_ref, acc_ref, rows_ref):
    j = pl.program_id(0)

    @pl.when(j == 0)
    def _():
        sign = jnp.where(lax.broadcasted_iota(jnp.int32, (SLOTS * 8, 128), 0) % 8 < 4, -1.0, 1.0)
        for ty in range(8):
            g, half = ty // 2, ty % 2
            plain = cur_ref[pl.ds(ty, SLOTS * 8, stride=8), :]
            swapped = pltpu.roll(plain.reshape(SLOTS, 8, 128), 4, 1).reshape(SLOTS * 8, 128) * sign
            rows = slice(g * SLOTS * 8, (g + 1) * SLOTS * 8)
            lhs_ref[rows, half * 128 : half * 128 + 128] = plain.astype(jnp.bfloat16)
            lhs_ref[rows, 256 + half * 128 : 384 + half * 128] = swapped.astype(jnp.bfloat16)

    for k in range(PER_STEP):
        far_block(scale, j * PER_STEP + k, k, lhs_ref, table_ref, weight_ref, acc_ref)

    @pl.when(j == pl.num_programs(0) - 1)
    def _():
        turned = acc_ref[...].T
        rows_ref[pl.ds(0, 256, stride=2), :] = turned[:, 0:128]
        rows_ref[pl.ds(1, 256, stride=2), :] = turned[:, 128:256]
        out_ref[...] = rows_ref[...].astype(out_ref.dtype)


def far_block(scale, j, k, lhs_ref, table_ref, weight_ref, acc_ref):
    prod = jnp.dot(lhs_ref[...], table_ref[k], preferred_element_type=jnp.float32)
    first = jnp.zeros((8, 256), jnp.float32)
    second = jnp.zeros((8, 256), jnp.float32)
    for g in range(4):
        for t in range(SLOTS):
            row = 8 * (g * SLOTS + t)
            piece = prod[row : row + 8]
            first = first + piece * weight_ref[k, 0, pl.ds(24 * g + t, 8, stride=0), :]
            second = second + piece * weight_ref[k, 1, pl.ds(24 * g + t, 8, stride=0), :]
    sign = jnp.where(lax.broadcasted_iota(jnp.int32, (8, 256), 0) < 4, -scale, scale)
    acc_ref[pl.ds(pl.multiple_of(j * 8, 8), 8), :] = first * scale + pltpu.roll(second, 4, 0) * sign


def far_products(currents, table, weight, scale, dtype):
    return pl.pallas_call(
        functools.partial(far_kernel, scale),
        grid=(32 // PER_STEP,),
        out_shape=jax.ShapeDtypeStruct((512, 128), dtype),
        in_specs=[
            pl.BlockSpec((SLOTS * 64, 128), lambda j: (0, 0)),
            pl.BlockSpec((PER_STEP, 512, 256), lambda j: (j, 0, 0)),
            pl.BlockSpec((PER_STEP, 2, 96, 256), lambda j: (j, 0, 0, 0)),
        ],
        out_specs=pl.BlockSpec((512, 128), lambda j: (0, 0)),
        scratch_shapes=[
            pltpu.VMEM((4 * SLOTS * 8, 512), jnp.bfloat16),
            pltpu.VMEM((256, 256), jnp.float32),
            pltpu.VMEM((512, 128), jnp.float32),
        ],
        cost_estimate=pl.CostEstimate(flops=5000000000, bytes_accessed=15000000, transcendentals=0),
        compiler_params=kernel_options(12),
        name="far",
    )(currents, table, weight)


def sum_kernel(in_ref, out_ref):
    eight = jnp.sum(in_ref[...].astype(jnp.float32).reshape(64, 8, 128), axis=0)
    halves = [sum(eight[k : k + 1] for k in range(h + 2, 8, 2)) + eight[h : h + 1] for h in range(2)]
    total = jnp.concatenate(halves, axis=1)
    row = lax.broadcasted_iota(jnp.int32, (8, 256), 0)
    col = lax.broadcasted_iota(jnp.int32, (8, 256), 1) % 8
    spread = jnp.where((row % 2) * 4 + row // 2 == col, jnp.broadcast_to(total, (8, 256)), 0.0)
    pick = jnp.where(
        lax.broadcasted_iota(jnp.int32, (256, 32), 0) // 8
        == lax.broadcasted_iota(jnp.int32, (256, 32), 1),
        1.0,
        0.0,
    )
    out_ref[...] = jnp.dot(
        spread, pick, preferred_element_type=jnp.float32, precision=lax.Precision.HIGHEST
    )


def sum_sources(received):
    return pl.pallas_call(
        sum_kernel,
        out_shape=jax.ShapeDtypeStruct((8, 32), jnp.float32),
        in_specs=[whole()],
        out_specs=whole(),
        compiler_params=kernel_options(4),
        name="sum_sources",
    )(received).T


def shards(
    fields,
    polarization,
    material,
    omega0,
    damping,
    strength,
    tile_count,
    tile_place,
    dir_angles,
    dir_order,
):
    sizes = tuple(lax.axis_size(axis) * n for axis, n in zip(AXES, fields.shape[1:]))
    index = jnp.stack([lax.axis_index(axis) for axis in AXES]).astype(jnp.int32)
    ints = jnp.concatenate([tile_place.reshape(-1), tile_count.reshape(-1), index])
    medium = jnp.concatenate([omega0, damping, strength])
    fields_out, currents, table, weight = window(
        fields, polarization, material, medium, ints, sizes, dir_angles, dir_order
    )
    tile_total = math.prod(lax.axis_size(axis) for axis in AXES) * TILE_MEAN
    scale = 1.0 / math.sqrt(tile_total * TY * fields.shape[3])
    partial = far_products(currents, table, weight, scale, jnp.bfloat16)
    received = lax.all_to_all(partial, AXES, 0, 0, tiled=True)
    return fields_out, sum_sources(received)


def solution(mesh):
    return jax.shard_map(
        shards,
        mesh=mesh,
        in_specs=(
            P(None, *AXES),
            P(None, *AXES),
            P(*AXES),
            P(),
            P(),
            P(),
            P(("gx", "gy"), None),
            P(("gx", "gy"), None, None),
            P(),
            P(),
        ),
        out_specs=(P(None, *AXES), P(AXES, None)),
        check_vma=False,
    )
```

```python
import functools
import math

import jax
import jax.numpy as jnp
from jax import lax
from jax.experimental import pallas as pl
from jax.experimental.pallas import tpu as pltpu
from jax.sharding import PartitionSpec as P

TY = 8
STEPS = 4
TILE_MEAN = 6
SLOTS = 18
SPEED = 0.5
WAVE = 0.35
HALO = jnp.bfloat16
LAG = 4
PER_STEP = 8
AXES = ("gx", "gy", "gz")


def whole():
    return pl.BlockSpec(memory_space=pltpu.VMEM)


def scalars():
    return pl.BlockSpec(memory_space=pltpu.SMEM)


def pack_depth_kernel(fields_ref, pol_ref, mat_ref, out_ref, buf_ref, raw_ref, sems):
    lane = lax.broadcasted_iota(jnp.int32, (16, 128), 1) // 8
    copies = [pltpu.make_async_copy(fields_ref.at[a], buf_ref.at[a], sems.at[a]) for a in range(6)]
    copies += [
        pltpu.make_async_copy(pol_ref.at[a], buf_ref.at[a + 6], sems.at[a + 6]) for a in range(6)
    ]
    copies.append(pltpu.make_async_copy(mat_ref, raw_ref, sems.at[12]))
    for copy in copies:
        copy.start()
    for a, copy in enumerate(copies):
        copy.wait()
        acc = jnp.zeros((16, 128), jnp.float32)
        for x in range(16):
            plane = raw_ref[x].astype(jnp.float32) if a == 12 else buf_ref[a, x]
            acc = jnp.where(lane == x, pltpu.roll(plane, (8 * x + 4) % 128, 1), acc)
        out_ref[a] = acc.astype(HALO)


def stage_kernel(fields_ref, pol_ref, mat_ref, own_ref):
    own_ref[0:6] = fields_ref[...]
    own_ref[6:12] = pol_ref[...]
    own_ref[12] = mat_ref[...].astype(jnp.float32)


def join_depth(before, after):
    lane = lax.broadcasted_iota(jnp.int32, (16, 128), 1) % 8
    return jnp.where(lane < 4, before.astype(jnp.float32), after.astype(jnp.float32))


def pack_x_kernel(own_ref, before_ref, after_ref, low_ref, high_ref):
    def body(a, carry):
        for k in range(3):
            low_ref[a * 3 + k] = own_ref[a, k].astype(HALO)
            high_ref[a * 3 + k] = own_ref[a, 13 + k].astype(HALO)
        return carry

    lax.fori_loop(0, 13, body, 0)
    for k, a in enumerate((1, 2)):
        low_ref[39 + k] = own_ref[a, 3].astype(HALO)
    for k, a in enumerate((0, 1, 2, 4, 5)):
        high_ref[39 + k] = own_ref[a, 12].astype(HALO)
    group = lax.broadcasted_iota(jnp.int32, (16, 128), 1) // 32
    for q in range(4):
        low = jnp.zeros((16, 128), jnp.float32)
        high = low
        for r in range(min(4, 13 - 4 * q)):
            depth = join_depth(before_ref[4 * q + r], after_ref[4 * q + r])
            low = jnp.where(group == r, pltpu.roll(depth, 32 * r, 1) if r else depth, low)
            high = jnp.where(group == r, pltpu.roll(depth, 32 * r + 32, 1) if r < 3 else depth, high)
        low_ref[41 + q] = low.astype(HALO)
        high_ref[44 + q] = high.astype(HALO)


def wide_plane(x, a, own_ref, before_ref, after_ref, left_ref, right_ref):
    if x < 16:
        return own_ref[a, x]
    if x < 19:
        return right_ref[a * 3 + x - 16].astype(jnp.float32)
    if x == 19:
        return right_ref[39 + min(max(a - 1, 0), 1)].astype(jnp.float32)
    if x == 20:
        return left_ref[39 + min(a if a < 3 else a - 1, 4)].astype(jnp.float32)
    if x < 24:
        return left_ref[a * 3 + x - 21].astype(jnp.float32)
    if x == 24:
        return join_depth(before_ref[a], after_ref[a])
    lane = lax.broadcasted_iota(jnp.int32, (16, 128), 1)
    turn = 32 * (a % 4)
    return jnp.where(
        lane < 32,
        pltpu.roll(right_ref[41 + a // 4].astype(jnp.float32), (128 - turn) % 128, 1),
        pltpu.roll(left_ref[44 + a // 4].astype(jnp.float32), (160 - turn) % 128, 1),
    )


def pack_y_kernel(
    own_ref, before_ref, after_ref, left_ref, right_ref, u_ref, low_ref, high_ref
):
    top = lax.broadcasted_iota(jnp.int32, (8, 128), 0) < 4

    for a in range(13):
        for i in range(13):
            p0, p1 = [
                wide_plane(2 * i + k, a, own_ref, before_ref, after_ref, left_ref, right_ref)
                for k in range(2)
            ]
            low_ref[a, i] = jnp.where(top, p0[0:8], pltpu.roll(p1[0:8], 4, 0)).astype(HALO)
            high_ref[a, i] = jnp.where(top, pltpu.roll(p1[8:16], 4, 0), p0[8:16]).astype(HALO)


def side_lanes(depth, x):
    return pltpu.roll(depth[x // 16], (124 - 8 * x) % 128, 1)


def coefficients(medium_ref, value):
    shape = value.shape
    a = jnp.zeros(shape, jnp.float32)
    b, c = a, a
    for m in range(4):
        omega = jnp.full((8, 128), medium_ref[m], jnp.float32)
        half = 0.5 * jnp.full((8, 128), medium_ref[4 + m], jnp.float32)
        strong = jnp.full((8, 128), medium_ref[8 + m], jnp.float32)
        square = omega * omega
        under = 1.0 + half
        hit = value == float(m + 1)
        wide = (lambda v: jnp.broadcast_to(jnp.concatenate([v[0:1]] * 2, axis=1), shape))
        a = jnp.where(hit, wide((2.0 - square) / under), a)
        b = jnp.where(hit, wide(-(1.0 - half) / under), b)
        c = jnp.where(hit, wide(strong * square / under), c)
    return a, b, c, jnp.where(value > 0.0, 1.0, 0.0)


def lay_kernel(
    medium_ref, own_ref, before_ref, after_ref, left_ref, right_ref, low_ref, wide_ref, coef_ref
):
    def spread(a, store):
        depth = [
            wide_plane(24 + k, a, own_ref, before_ref, after_ref, left_ref, right_ref)
            for k in range(2)
        ]
        for x in range(24):
            main = wide_plane(x, a, own_ref, before_ref, after_ref, left_ref, right_ref)
            store(x, jnp.concatenate([main, side_lanes(depth, x)], axis=1))

    for a in range(12):

        def store(x, value, a=a):
            wide_ref[a, x] = value

        spread(a, store)

    def store_coef(x, value):
        for k, coef in enumerate(coefficients(medium_ref, value)):
            coef_ref[k, x] = coef

    spread(12, store_coef)


def window_kernel(
    extents,
    ints_ref,
    medium_ref,
    laid_ref,
    laid_coef_ref,
    down_ref,
    up_ref,
    out_ref,
    cur_ref,
    wide_ref,
    tail_ref,
    tail_coef_ref,
    phasor_ref,
    final_ref,
    sems,
):
    top = lax.broadcasted_iota(jnp.int32, (8, 128), 0) < 4

    def spread(a, store):
        def rows(i):
            lowest = up_ref[a, i].astype(jnp.float32)
            highest = down_ref[a, i].astype(jnp.float32)
            return (
                jnp.where(top, lowest, highest),
                pltpu.roll(jnp.where(top, highest, lowest), 4, 0),
            )

        depth = rows(12)
        for i in range(12):
            tail = rows(i)
            for k in range(2):
                x = 2 * i + k
                store(x, jnp.concatenate([tail[k], side_lanes(depth, x)], axis=1))

    for a in range(12):

        def store(x, value, a=a):
            tail_ref[a, x] = value

        spread(a, store)

    def store_coef(x, value):
        for k, coef in enumerate(coefficients(medium_ref, value)):
            tail_coef_ref[k, x] = coef

    spread(12, store_coef)

    def first_value(k, x):
        return jnp.concatenate([laid_ref[k, x], tail_ref[k, x]], axis=0)

    def coefficient(k, x):
        return jnp.concatenate([laid_coef_ref[k, x], tail_coef_ref[k, x]], axis=0)

    gx, gy, gz = ints_ref[76], ints_ref[77], ints_ref[78]
    row = lax.broadcasted_iota(jnp.int32, (24, 256), 0)
    row = jnp.where(row < 20, row, row - 24) + gy * 16
    lane = lax.broadcasted_iota(jnp.int32, (24, 256), 1)
    near = (lane < 132) | (lane >= 252)
    lane = jnp.where(lane < 132, lane, lane - 256) + gz * 128
    inside = near & (row >= 0) & (row < extents[1]) & (lane >= 0) & (lane < extents[2])
    inside = jnp.where(inside, SPEED, 0.0).astype(jnp.float32)

    def ahead_y(v):
        return pltpu.roll(v, 23, 0)

    def behind_y(v):
        return pltpu.roll(v, 1, 0)

    def ahead_z(v):
        return pltpu.roll(v, 255, 1)

    def behind_z(v):
        return pltpu.roll(v, 1, 1)

    for k in (4, 5):
        wide_ref[k, 19] = jnp.zeros((24, 256), jnp.float32)

    def wrap(x):
        return x % 24

    def magnetic_step(n, x):
        here, after = wrap(x), wrap(x + 1)
        place = gx * 16 + x
        speed = inside
        if not 0 <= x < 16:
            speed = inside * jnp.where((place >= 0) & (place < extents[0]), 1.0, 0.0)
        get = first_value if n == 0 else (lambda k, at: wide_ref[k, at])
        ex, ey, ez = get(0, here), get(1, here), get(2, here)
        ey_next, ez_next = get(1, after), get(2, after)
        hx = get(3, here) - speed * ((ahead_y(ez) - ez) - (ahead_z(ey) - ey))
        hy = get(4, here) - speed * ((ahead_z(ex) - ex) - (ez_next - ez))
        hz = get(5, here) - speed * ((ey_next - ey) - (ahead_y(ex) - ex))
        wide_ref[3, here] = hx
        wide_ref[4, here] = hy
        wide_ref[5, here] = hz
        return speed, hx, hy, hz

    def electric_step(n, x, inner, speed, hx, hy, hz):
        here, prior = wrap(x), wrap(x - 1)
        last = n == STEPS - 1

        def cut(v):
            return v[0:16, 0:128] if last else v

        now, old = (6, 9) if n % 2 == 0 else (9, 6)

        def get(k, at, fresh=True):
            if fresh and (n == 0 or (n == 1 and k >= 6 and k < 9)):
                return first_value(k, at)
            return wide_ref[k, at, 0:16, 0:128] if last else wide_ref[k, at]

        def get_coef(k):
            return laid_coef_ref[k, here, 0:16, 0:128] if last else coefficient(k, here)

        def put(k, value):
            if last:
                wide_ref[k, here, 0:16, 0:128] = value
            else:
                wide_ref[k, here] = value

        ex, ey, ez = get(0, here), get(1, here), get(2, here)
        hy_prior, hz_prior = get(4, prior, False), get(5, prior, False)
        sat = 1.0 / (1.0 + ex * ex + ey * ey + ez * ez)
        a, b, sheet = get_coef(0), get_coef(1), get_coef(3)
        drive = get_coef(2) * sat
        hxc, hyc, hzc = cut(hx), cut(hy), cut(hz)
        curls = (
            (hzc - cut(behind_y(hz))) - (hyc - cut(behind_z(hy))),
            (hxc - cut(behind_z(hx))) - (hzc - hz_prior),
            (hyc - hy_prior) - (hxc - cut(behind_y(hx))),
        )
        rate = cut(speed)
        fresh = []
        for c, e in enumerate((ex, ey, ez)):
            pol = get(now + c, here)
            pol_new = a * pol + b * get(old + c, here) + drive * e
            value = e + rate * curls[c] - sheet * (pol_new - pol)
            if last:
                final_ref[c, x] = value
            else:
                put(old + c, pol_new)
                put(c, value)
            fresh.append(value)
        if inner:
            angle_h = WAVE * SPEED * (n + 0.5)
            angle_e = WAVE * SPEED * (n + 1.0)
            hxc, hyc, hzc = hx[0:16, 0:128], hy[0:16, 0:128], hz[0:16, 0:128]
            ey, ez = fresh[1][0:16, 0:128], fresh[2][0:16, 0:128]
            terms = (
                (-math.cos(angle_h), hzc),
                (math.cos(angle_h), hyc),
                (math.cos(angle_e), ez),
                (-math.cos(angle_e), ey),
                (math.sin(angle_h), hzc),
                (-math.sin(angle_h), hyc),
                (-math.sin(angle_e), ez),
                (math.sin(angle_e), ey),
            )
            for o, (factor, value) in enumerate(terms):
                phasor_ref[o, x] = factor * value if n == 0 else phasor_ref[o, x] + factor * value
            if last:
                final_ref[3, x] = hxc
                final_ref[4, x] = hyc
                final_ref[5, x] = hzc

    copies = []
    for n in range(STEPS):
        planes = list(range(n - 4, 19 - n))
        states = {}
        for k in range(len(planes) + LAG):
            if k < len(planes):
                states[planes[k]] = magnetic_step(n, planes[k])
            if k >= LAG:
                x = planes[k - LAG]
                inner = 0 <= x < 16
                if inner or n < STEPS - 1:
                    electric_step(n, x, inner, *states.pop(x))
                if n == STEPS - 1 and inner and x % 4 == 3:
                    part = pl.ds(x - 3, 4)
                    copies.append(
                        pltpu.make_async_copy(
                            final_ref.at[:, part], out_ref.at[:, part], sems.at[x // 4]
                        )
                    )
                    copies[-1].start()

    count = ints_ref[72 + gz]

    def put_tile(t, carry):
        p = ints_ref[gz * SLOTS + t]
        live = jnp.where(t < count, 1.0, 0.0)
        rows = pl.ds(pl.multiple_of((p & 1) * 8, 8), 8)
        for o in range(8):
            cur_ref[pl.ds(pl.multiple_of(t * 64 + o * 8, 8), 8), :] = phasor_ref[o, p >> 1, rows, :] * live
        return carry

    lax.fori_loop(0, SLOTS, put_tile, 0)
    for copy in copies:
        copy.wait()


def kernel_options(mib):
    return pltpu.CompilerParams(vmem_limit_bytes=mib << 20)


def shift(block, axis, by):
    count = lax.axis_size(axis)
    pairs = [(i, i + by) for i in range(count) if 0 <= i + by < count]
    return lax.ppermute(block, axis, pairs)


def window(fields, polarization, material, medium, ints, sizes, dir_angles, dir_order):
    anywhere = pl.BlockSpec(memory_space=pl.ANY)
    depth = pl.pallas_call(
        pack_depth_kernel,
        out_shape=jax.ShapeDtypeStruct((13, 16, 128), HALO),
        in_specs=[pl.BlockSpec(memory_space=pltpu.HBM)] * 3,
        out_specs=whole(),
        scratch_shapes=[
            pltpu.VMEM((12, 16, 16, 128), jnp.float32),
            pltpu.VMEM((16, 16, 128), jnp.int32),
            pltpu.SemaphoreType.DMA((13,)),
        ],
        compiler_params=pltpu.CompilerParams(vmem_limit_bytes=65000 << 10),
        name="pack_depth",
    )(fields, polarization, material)
    later, _ = lax.optimization_barrier(((fields, polarization, material), depth))
    own = pl.pallas_call(
        stage_kernel,
        out_shape=jax.ShapeDtypeStruct((13, 16, 16, 128), jnp.float32),
        in_specs=[whole()] * 3,
        out_specs=whole(),
        compiler_params=kernel_options(6),
        name="stage",
    )(*later)
    before, after = shift(depth, "gz", 1), shift(depth, "gz", -1)
    low, high = pl.pallas_call(
        pack_x_kernel,
        out_shape=(
            jax.ShapeDtypeStruct((45, 16, 128), HALO),
            jax.ShapeDtypeStruct((48, 16, 128), HALO),
        ),
        in_specs=[whole()] * 3,
        out_specs=(whole(),) * 2,
        compiler_params=kernel_options(6),
        name="pack_x",
    )(own, before, after)
    left, right = shift(high, "gx", 1), shift(low, "gx", -1)
    u = directions(dir_angles, dir_order, low)
    table, weight = tables(u, ints, low)
    low, high = pl.pallas_call(
        pack_y_kernel,
        out_shape=(jax.ShapeDtypeStruct((13, 13, 8, 128), HALO),) * 2,
        in_specs=[whole()] * 5 + [anywhere],
        out_specs=(whole(),) * 2,
        compiler_params=kernel_options(6),
        name="pack_y",
    )(own, before, after, left, right, weight)
    laid, laid_coef = pl.pallas_call(
        lay_kernel,
        out_shape=(
            jax.ShapeDtypeStruct((12, 24, 16, 256), jnp.float32),
            jax.ShapeDtypeStruct((4, 24, 16, 256), jnp.float32),
        ),
        in_specs=[scalars()] + [whole()] * 5 + [anywhere],
        out_specs=(whole(),) * 2,
        compiler_params=kernel_options(10),
        cost_estimate=pl.CostEstimate(flops=8000000, bytes_accessed=9000000, transcendentals=0),
        name="lay",
    )(medium, own, before, after, left, right, low)
    down, up = shift(high, "gy", 1), shift(low, "gy", -1)
    fields_out, currents = pl.pallas_call(
        functools.partial(window_kernel, sizes),
        out_shape=(
            jax.ShapeDtypeStruct((6, 16, 16, 128), jnp.float32),
            jax.ShapeDtypeStruct((SLOTS * 64, 128), jnp.float32),
        ),
        in_specs=[scalars()] * 2 + [whole()] * 4,
        out_specs=(anywhere, whole()),
        scratch_shapes=[
            pltpu.VMEM((12, 24, 24, 256), jnp.float32),
            pltpu.VMEM((12, 24, 8, 256), jnp.float32),
            pltpu.VMEM((4, 24, 8, 256), jnp.float32),
            pltpu.VMEM((8, 16, 16, 128), jnp.float32),
            pltpu.VMEM((6, 16, 16, 128), jnp.float32),
            pltpu.SemaphoreType.DMA((4,)),
        ],
        compiler_params=kernel_options(24),
        name="window",
    )(ints, medium, laid, laid_coef, down, up)
    return fields_out, currents, table, weight


TWO_PI = 2.0 * math.pi
TURN = 0.35 / TWO_PI
PAIRS = 4 * SLOTS


def sin_quarter(y):
    z = y * y
    c = [TWO_PI ** n * s / math.factorial(n) for n, s in ((1, 1), (3, -1), (5, 1), (7, -1), (9, 1), (11, -1))]
    acc = jnp.full_like(z, c[5])
    for k in (4, 3, 2, 1, 0):
        acc = acc * z + c[k]
    return acc * y


def cos_sin(turns):
    r = turns - jnp.floor(turns + 0.5)
    a = jnp.abs(r)
    cos = sin_quarter(0.25 - a)
    sin = sin_quarter(0.25 - jnp.abs(a - 0.25))
    return cos, jnp.where(r < 0, -sin, sin)


def dirs_kernel(angles_ref, order_ref, low_ref, u_ref):
    idx = order_ref[...]
    hi = idx >> 7
    lo = idx & 127

    def body(h, acc):
        polar, azim = acc
        pick = hi == h
        row_p = jnp.broadcast_to(angles_ref[0, pl.ds(h, 1), :], lo.shape)
        row_a = jnp.broadcast_to(angles_ref[1, pl.ds(h, 1), :], lo.shape)
        polar = jnp.where(pick, jnp.take_along_axis(row_p, lo, axis=1), polar)
        azim = jnp.where(pick, jnp.take_along_axis(row_a, lo, axis=1), azim)
        return polar, azim

    zero = jnp.zeros(idx.shape, jnp.float32)
    polar, azim = lax.fori_loop(0, 64, body, (zero, zero), unroll=4)
    cos_p, sin_p = cos_sin(polar * (1.0 / TWO_PI))
    cos_a, sin_a = cos_sin(azim * (1.0 / TWO_PI))
    u_ref[0] = sin_p * cos_a
    u_ref[1] = sin_p * sin_a
    u_ref[2] = cos_p


def directions(dir_angles, dir_order, low):
    order = dir_order.reshape(256, 32).T.reshape(64, 128)
    return pl.pallas_call(
        dirs_kernel,
        out_shape=jax.ShapeDtypeStruct((3, 64, 128), jnp.float32),
        in_specs=[whole(), whole(), pl.BlockSpec(memory_space=pl.ANY)],
        out_specs=whole(),
        cost_estimate=pl.CostEstimate(flops=3000000, bytes_accessed=300000, transcendentals=0),
        compiler_params=kernel_options(12),
        name="dirs",
    )(dir_angles.reshape(2, 64, 128), order, low)


def tables_kernel(ints_ref, low_ref, u_ref, table_ref, weight_ref, pos_ref):
    @pl.when(pl.program_id(0) == 0)
    def _():
        gx, gy, gz = ints_ref[76], ints_ref[77], ints_ref[78]
        pos_ref[...] = jnp.zeros_like(pos_ref)
        for t in range(SLOTS):
            p = ints_ref[gz * SLOTS + t]
            for axis, start in enumerate((gx * 16 + (p >> 1), gy * 16 + (p & 1) * 8, gz * 128)):
                pos_ref[axis, t : t + 1, :] = jnp.full((1, 256), start.astype(jnp.float32))

    j2 = pl.multiple_of(pl.program_id(0) * 2, 2)

    def row(axis):
        return jnp.concatenate(
            [u_ref[axis, pl.ds(j2, 1), :], u_ref[axis, pl.ds(j2 + 1, 1), :]], axis=1
        ) * TURN

    ux, uy, uz = row(0), row(1), row(2)
    eight = lax.broadcasted_iota(jnp.int32, (8, 256), 0).astype(jnp.float32)
    sixteen = lax.broadcasted_iota(jnp.int32, (16, 256), 0).astype(jnp.float32) * 8.0
    low_c, low_s = cos_sin(uz * eight)
    high_c, high_s = cos_sin(uz * sixteen)
    row_c, row_s = cos_sin(uy * eight)
    one_c, one_s = row_c[1:2], row_s[1:2]
    for pair in range(8):
        rows = ([], [], [], [])
        for half in range(2):
            a = 2 * pair + half
            hc, hs = high_c[a : a + 1], high_s[a : a + 1]
            c = hc * low_c - hs * low_s
            s = hs * low_c + hc * low_s
            rows[0].append(c)
            rows[1].append(c * one_c - s * one_s)
            rows[2].append(s)
            rows[3].append(s * one_c + c * one_s)
        for part in range(4):
            table_ref[0, part * 128 + 16 * pair : part * 128 + 16 * pair + 16, :] = jnp.concatenate(
                rows[part], axis=0
            ).astype(jnp.bfloat16)
    phase = pos_ref[0] * ux + pos_ref[1] * uy + pos_ref[2] * uz
    tile_c, tile_s = cos_sin(phase)
    for g in range(4):
        gc, gs = row_c[2 * g : 2 * g + 1], row_s[2 * g : 2 * g + 1]
        weight_ref[0, 0, 24 * g : 24 * g + 24, :] = tile_c * gc - tile_s * gs
        weight_ref[0, 1, 24 * g : 24 * g + 24, :] = tile_s * gc + tile_c * gs


def tables(u, ints, low):
    return pl.pallas_call(
        tables_kernel,
        grid=(32,),
        out_shape=(
            jax.ShapeDtypeStruct((32, 512, 256), jnp.bfloat16),
            jax.ShapeDtypeStruct((32, 2, 104, 256), jnp.float32),
        ),
        in_specs=[
            scalars(),
            pl.BlockSpec(memory_space=pl.ANY),
            pl.BlockSpec((3, 64, 128), lambda j: (0, 0, 0)),
        ],
        out_specs=(
            pl.BlockSpec((1, 512, 256), lambda j: (j, 0, 0)),
            pl.BlockSpec((1, 2, 104, 256), lambda j: (j, 0, 0, 0)),
        ),
        scratch_shapes=[pltpu.VMEM((3, 24, 256), jnp.float32)],
        cost_estimate=pl.CostEstimate(flops=60000000, bytes_accessed=14000000, transcendentals=0),
        compiler_params=kernel_options(12),
        name="tables",
    )(ints, low, u)


def far_kernel(scale, cur_ref, table_ref, weight_ref, out_ref, lhs_ref, acc_ref, rows_ref):
    j = pl.program_id(0)

    @pl.when(j == 0)
    def _():
        sign = jnp.where(lax.broadcasted_iota(jnp.int32, (SLOTS * 8, 128), 0) % 8 < 4, -1.0, 1.0)
        for ty in range(8):
            g, half = ty // 2, ty % 2
            plain = cur_ref[pl.ds(ty, SLOTS * 8, stride=8), :]
            swapped = pltpu.roll(plain.reshape(SLOTS, 8, 128), 4, 1).reshape(SLOTS * 8, 128) * sign
            rows = slice(g * SLOTS * 8, (g + 1) * SLOTS * 8)
            lhs_ref[rows, half * 128 : half * 128 + 128] = plain.astype(jnp.bfloat16)
            lhs_ref[rows, 256 + half * 128 : 384 + half * 128] = swapped.astype(jnp.bfloat16)

    for k in range(PER_STEP):
        far_block(scale, j * PER_STEP + k, k, lhs_ref, table_ref, weight_ref, acc_ref)

    @pl.when(j == pl.num_programs(0) - 1)
    def _():
        turned = acc_ref[...].T
        rows_ref[pl.ds(0, 256, stride=2), :] = turned[:, 0:128]
        rows_ref[pl.ds(1, 256, stride=2), :] = turned[:, 128:256]
        out_ref[...] = rows_ref[...].astype(out_ref.dtype)


def far_block(scale, j, k, lhs_ref, table_ref, weight_ref, acc_ref):
    prod = jnp.dot(lhs_ref[...], table_ref[k], preferred_element_type=jnp.float32)
    first = jnp.zeros((8, 256), jnp.float32)
    second = jnp.zeros((8, 256), jnp.float32)
    for g in range(4):
        for t in range(SLOTS):
            row = 8 * (g * SLOTS + t)
            piece = prod[row : row + 8]
            first = first + piece * weight_ref[k, 0, pl.ds(24 * g + t, 8, stride=0), :]
            second = second + piece * weight_ref[k, 1, pl.ds(24 * g + t, 8, stride=0), :]
    sign = jnp.where(lax.broadcasted_iota(jnp.int32, (8, 256), 0) < 4, -scale, scale)
    acc_ref[pl.ds(pl.multiple_of(j * 8, 8), 8), :] = first * scale + pltpu.roll(second, 4, 0) * sign


def far_products(currents, table, weight, scale, dtype):
    return pl.pallas_call(
        functools.partial(far_kernel, scale),
        grid=(32 // PER_STEP,),
        out_shape=jax.ShapeDtypeStruct((512, 128), dtype),
        in_specs=[
            pl.BlockSpec((SLOTS * 64, 128), lambda j: (0, 0)),
            pl.BlockSpec((PER_STEP, 512, 256), lambda j: (j, 0, 0)),
            pl.BlockSpec((PER_STEP, 2, 104, 256), lambda j: (j, 0, 0, 0)),
        ],
        out_specs=pl.BlockSpec((512, 128), lambda j: (0, 0)),
        scratch_shapes=[
            pltpu.VMEM((4 * SLOTS * 8, 512), jnp.bfloat16),
            pltpu.VMEM((256, 256), jnp.float32),
            pltpu.VMEM((512, 128), jnp.float32),
        ],
        cost_estimate=pl.CostEstimate(flops=5000000000, bytes_accessed=15000000, transcendentals=0),
        compiler_params=kernel_options(12),
        name="far",
    )(currents, table, weight)


def sum_kernel(in_ref, out_ref):
    eight = jnp.sum(in_ref[...].astype(jnp.float32).reshape(64, 8, 128), axis=0)
    halves = [sum(eight[k : k + 1] for k in range(h + 2, 8, 2)) + eight[h : h + 1] for h in range(2)]
    total = jnp.concatenate(halves, axis=1)
    row = lax.broadcasted_iota(jnp.int32, (8, 256), 0)
    col = lax.broadcasted_iota(jnp.int32, (8, 256), 1) % 8
    spread = jnp.where((row % 2) * 4 + row // 2 == col, jnp.broadcast_to(total, (8, 256)), 0.0)
    pick = jnp.where(
        lax.broadcasted_iota(jnp.int32, (256, 32), 0) // 8
        == lax.broadcasted_iota(jnp.int32, (256, 32), 1),
        1.0,
        0.0,
    )
    out_ref[...] = jnp.dot(
        spread, pick, preferred_element_type=jnp.float32, precision=lax.Precision.HIGHEST
    )


def sum_sources(received):
    return pl.pallas_call(
        sum_kernel,
        out_shape=jax.ShapeDtypeStruct((8, 32), jnp.float32),
        in_specs=[whole()],
        out_specs=whole(),
        compiler_params=kernel_options(4),
        name="sum_sources",
    )(received).T


def shards(
    fields,
    polarization,
    material,
    omega0,
    damping,
    strength,
    tile_count,
    tile_place,
    dir_angles,
    dir_order,
):
    sizes = tuple(lax.axis_size(axis) * n for axis, n in zip(AXES, fields.shape[1:]))
    index = jnp.stack([lax.axis_index(axis) for axis in AXES]).astype(jnp.int32)
    ints = jnp.concatenate([tile_place.reshape(-1), tile_count.reshape(-1), index])
    medium = jnp.concatenate([omega0, damping, strength])
    fields_out, currents, table, weight = window(
        fields, polarization, material, medium, ints, sizes, dir_angles, dir_order
    )
    tile_total = math.prod(lax.axis_size(axis) for axis in AXES) * TILE_MEAN
    scale = 1.0 / math.sqrt(tile_total * TY * fields.shape[3])
    partial = far_products(currents, table, weight, scale, jnp.bfloat16)
    received = lax.all_to_all(partial, AXES, 0, 0, tiled=True)
    return fields_out, sum_sources(received)


def solution(mesh):
    return jax.shard_map(
        shards,
        mesh=mesh,
        in_specs=(
            P(None, *AXES),
            P(None, *AXES),
            P(*AXES),
            P(),
            P(),
            P(),
            P(("gx", "gy"), None),
            P(("gx", "gy"), None, None),
            P(),
            P(),
        ),
        out_specs=(P(None, *AXES), P(AXES, None)),
        check_vma=False,
    )
```

```python
import functools
import math

import jax
import jax.numpy as jnp
from jax import lax
from jax.experimental import pallas as pl
from jax.experimental.pallas import tpu as pltpu
from jax.sharding import PartitionSpec as P

TY = 8
STEPS = 4
TILE_MEAN = 6
SLOTS = 18
SPEED = 0.5
WAVE = 0.35
HALO = jnp.bfloat16
LAG = 4
PER_STEP = 8
AXES = ("gx", "gy", "gz")


def whole():
    return pl.BlockSpec(memory_space=pltpu.VMEM)


def scalars():
    return pl.BlockSpec(memory_space=pltpu.SMEM)


def pack_depth_kernel(fields_ref, pol_ref, mat_ref, out_ref, buf_ref, raw_ref, sems):
    lane = lax.broadcasted_iota(jnp.int32, (16, 128), 1) // 8
    copies = [pltpu.make_async_copy(fields_ref.at[a], buf_ref.at[a], sems.at[a]) for a in range(6)]
    copies += [
        pltpu.make_async_copy(pol_ref.at[a], buf_ref.at[a + 6], sems.at[a + 6]) for a in range(6)
    ]
    copies.append(pltpu.make_async_copy(mat_ref, raw_ref, sems.at[12]))
    for copy in copies:
        copy.start()
    for a, copy in enumerate(copies):
        copy.wait()
        acc = jnp.zeros((16, 128), jnp.float32)
        for x in range(16):
            plane = raw_ref[x].astype(jnp.float32) if a == 12 else buf_ref[a, x]
            acc = jnp.where(lane == x, pltpu.roll(plane, (8 * x + 4) % 128, 1), acc)
        out_ref[a] = acc.astype(HALO)


def stage_kernel(fields_ref, pol_ref, mat_ref, own_ref):
    own_ref[0:6] = fields_ref[...]
    own_ref[6:12] = pol_ref[...]
    own_ref[12] = mat_ref[...].astype(jnp.float32)


def join_depth(before, after):
    lane = lax.broadcasted_iota(jnp.int32, (16, 128), 1) % 8
    return jnp.where(lane < 4, before.astype(jnp.float32), after.astype(jnp.float32))


def pack_x_kernel(own_ref, before_ref, after_ref, low_ref, high_ref):
    def body(a, carry):
        for k in range(3):
            low_ref[a * 3 + k] = own_ref[a, k].astype(HALO)
            high_ref[a * 3 + k] = own_ref[a, 13 + k].astype(HALO)
        return carry

    lax.fori_loop(0, 13, body, 0)
    for k, a in enumerate((1, 2)):
        low_ref[39 + k] = own_ref[a, 3].astype(HALO)
    for k, a in enumerate((0, 1, 2, 4, 5)):
        high_ref[39 + k] = own_ref[a, 12].astype(HALO)
    group = lax.broadcasted_iota(jnp.int32, (16, 128), 1) // 32
    for q in range(4):
        low = jnp.zeros((16, 128), jnp.float32)
        high = low
        for r in range(min(4, 13 - 4 * q)):
            depth = join_depth(before_ref[4 * q + r], after_ref[4 * q + r])
            low = jnp.where(group == r, pltpu.roll(depth, 32 * r, 1) if r else depth, low)
            high = jnp.where(group == r, pltpu.roll(depth, 32 * r + 32, 1) if r < 3 else depth, high)
        low_ref[41 + q] = low.astype(HALO)
        high_ref[44 + q] = high.astype(HALO)


def wide_plane(x, a, own_ref, before_ref, after_ref, left_ref, right_ref):
    if x < 16:
        return own_ref[a, x]
    if x < 19:
        return right_ref[a * 3 + x - 16].astype(jnp.float32)
    if x == 19:
        return right_ref[39 + min(max(a - 1, 0), 1)].astype(jnp.float32)
    if x == 20:
        return left_ref[39 + min(a if a < 3 else a - 1, 4)].astype(jnp.float32)
    if x < 24:
        return left_ref[a * 3 + x - 21].astype(jnp.float32)
    if x == 24:
        return join_depth(before_ref[a], after_ref[a])
    lane = lax.broadcasted_iota(jnp.int32, (16, 128), 1)
    turn = 32 * (a % 4)
    return jnp.where(
        lane < 32,
        pltpu.roll(right_ref[41 + a // 4].astype(jnp.float32), (128 - turn) % 128, 1),
        pltpu.roll(left_ref[44 + a // 4].astype(jnp.float32), (160 - turn) % 128, 1),
    )


def pack_y_kernel(
    own_ref, before_ref, after_ref, left_ref, right_ref, u_ref, low_ref, high_ref
):
    top = lax.broadcasted_iota(jnp.int32, (8, 128), 0) < 4

    for a in range(13):
        for i in range(13):
            p0, p1 = [
                wide_plane(2 * i + k, a, own_ref, before_ref, after_ref, left_ref, right_ref)
                for k in range(2)
            ]
            low_ref[a, i] = jnp.where(top, p0[0:8], pltpu.roll(p1[0:8], 4, 0)).astype(HALO)
            high_ref[a, i] = jnp.where(top, pltpu.roll(p1[8:16], 4, 0), p0[8:16]).astype(HALO)


def side_lanes(depth, x):
    return pltpu.roll(depth[x // 16], (124 - 8 * x) % 128, 1)


def coefficients(medium_ref, value):
    shape = value.shape
    a = jnp.zeros(shape, jnp.float32)
    b, c = a, a
    for m in range(4):
        omega = jnp.full((8, 128), medium_ref[m], jnp.float32)
        half = 0.5 * jnp.full((8, 128), medium_ref[4 + m], jnp.float32)
        strong = jnp.full((8, 128), medium_ref[8 + m], jnp.float32)
        square = omega * omega
        under = 1.0 + half
        hit = value == float(m + 1)
        wide = (lambda v: jnp.broadcast_to(jnp.concatenate([v[0:1]] * 2, axis=1), shape))
        a = jnp.where(hit, wide((2.0 - square) / under), a)
        b = jnp.where(hit, wide(-(1.0 - half) / under), b)
        c = jnp.where(hit, wide(strong * square / under), c)
    return a, b, c, jnp.where(value > 0.0, 1.0, 0.0)


def lay_kernel(
    medium_ref, own_ref, before_ref, after_ref, left_ref, right_ref, low_ref, wide_ref, coef_ref
):
    def spread(a, store):
        depth = [
            wide_plane(24 + k, a, own_ref, before_ref, after_ref, left_ref, right_ref)
            for k in range(2)
        ]
        for x in range(24):
            main = wide_plane(x, a, own_ref, before_ref, after_ref, left_ref, right_ref)
            store(x, jnp.concatenate([main, side_lanes(depth, x)], axis=1))

    for a in range(12):

        def store(x, value, a=a):
            wide_ref[a, x] = value

        spread(a, store)

    def store_coef(x, value):
        for k, coef in enumerate(coefficients(medium_ref, value)):
            coef_ref[k, x] = coef

    spread(12, store_coef)


def window_kernel(
    extents,
    ints_ref,
    medium_ref,
    laid_ref,
    laid_coef_ref,
    down_ref,
    up_ref,
    out_ref,
    cur_ref,
    wide_ref,
    tail_ref,
    tail_coef_ref,
    phasor_ref,
    final_ref,
    sems,
):
    top = lax.broadcasted_iota(jnp.int32, (8, 128), 0) < 4

    def spread(a, store):
        def rows(i):
            lowest = up_ref[a, i].astype(jnp.float32)
            highest = down_ref[a, i].astype(jnp.float32)
            return (
                jnp.where(top, lowest, highest),
                pltpu.roll(jnp.where(top, highest, lowest), 4, 0),
            )

        depth = rows(12)
        for i in range(12):
            tail = rows(i)
            for k in range(2):
                x = 2 * i + k
                store(x, jnp.concatenate([tail[k], side_lanes(depth, x)], axis=1))

    for a in range(12):

        def store(x, value, a=a):
            tail_ref[a, x] = value

        spread(a, store)

    def store_coef(x, value):
        for k, coef in enumerate(coefficients(medium_ref, value)):
            tail_coef_ref[k, x] = coef

    spread(12, store_coef)

    def first_value(k, x):
        return jnp.concatenate([laid_ref[k, x], tail_ref[k, x]], axis=0)

    def coefficient(k, x):
        return jnp.concatenate([laid_coef_ref[k, x], tail_coef_ref[k, x]], axis=0)

    gx, gy, gz = ints_ref[76], ints_ref[77], ints_ref[78]
    row = lax.broadcasted_iota(jnp.int32, (24, 256), 0)
    row = jnp.where(row < 20, row, row - 24) + gy * 16
    lane = lax.broadcasted_iota(jnp.int32, (24, 256), 1)
    near = (lane < 132) | (lane >= 252)
    lane = jnp.where(lane < 132, lane, lane - 256) + gz * 128
    inside = near & (row >= 0) & (row < extents[1]) & (lane >= 0) & (lane < extents[2])
    inside = jnp.where(inside, SPEED, 0.0).astype(jnp.float32)

    def ahead_y(v):
        return pltpu.roll(v, 23, 0)

    def behind_y(v):
        return pltpu.roll(v, 1, 0)

    def ahead_z(v):
        return pltpu.roll(v, 255, 1)

    def behind_z(v):
        return pltpu.roll(v, 1, 1)

    for k in (4, 5):
        wide_ref[k, 19] = jnp.zeros((24, 256), jnp.float32)

    def wrap(x):
        return x % 24

    def magnetic_step(n, x):
        here, after = wrap(x), wrap(x + 1)
        place = gx * 16 + x
        speed = inside
        if not 0 <= x < 16:
            speed = inside * jnp.where((place >= 0) & (place < extents[0]), 1.0, 0.0)
        get = first_value if n == 0 else (lambda k, at: wide_ref[k, at])
        ex, ey, ez = get(0, here), get(1, here), get(2, here)
        ey_next, ez_next = get(1, after), get(2, after)
        hx = get(3, here) - speed * ((ahead_y(ez) - ez) - (ahead_z(ey) - ey))
        hy = get(4, here) - speed * ((ahead_z(ex) - ex) - (ez_next - ez))
        hz = get(5, here) - speed * ((ey_next - ey) - (ahead_y(ex) - ex))
        wide_ref[3, here] = hx
        wide_ref[4, here] = hy
        wide_ref[5, here] = hz
        return speed, hx, hy, hz

    def electric_step(n, x, inner, speed, hx, hy, hz):
        here, prior = wrap(x), wrap(x - 1)
        last = n == STEPS - 1

        def cut(v):
            return v[0:16, 0:128] if last else v

        now, old = (6, 9) if n % 2 == 0 else (9, 6)

        def get(k, at, fresh=True):
            if fresh and (n == 0 or (n == 1 and k >= 6 and k < 9)):
                return first_value(k, at)
            return wide_ref[k, at, 0:16, 0:128] if last else wide_ref[k, at]

        def get_coef(k):
            return laid_coef_ref[k, here, 0:16, 0:128] if last else coefficient(k, here)

        def put(k, value):
            if last:
                wide_ref[k, here, 0:16, 0:128] = value
            else:
                wide_ref[k, here] = value

        ex, ey, ez = get(0, here), get(1, here), get(2, here)
        hy_prior, hz_prior = get(4, prior, False), get(5, prior, False)
        sat = 1.0 / (1.0 + ex * ex + ey * ey + ez * ez)
        a, b, sheet = get_coef(0), get_coef(1), get_coef(3)
        drive = get_coef(2) * sat
        hxc, hyc, hzc = cut(hx), cut(hy), cut(hz)
        curls = (
            (hzc - cut(behind_y(hz))) - (hyc - cut(behind_z(hy))),
            (hxc - cut(behind_z(hx))) - (hzc - hz_prior),
            (hyc - hy_prior) - (hxc - cut(behind_y(hx))),
        )
        rate = cut(speed)
        fresh = []
        for c, e in enumerate((ex, ey, ez)):
            pol = get(now + c, here)
            pol_new = a * pol + b * get(old + c, here) + drive * e
            value = e + rate * curls[c] - sheet * (pol_new - pol)
            if last:
                final_ref[c, x] = value
            else:
                put(old + c, pol_new)
                put(c, value)
            fresh.append(value)
        if inner:
            angle_h = WAVE * SPEED * (n + 0.5)
            angle_e = WAVE * SPEED * (n + 1.0)
            hxc, hyc, hzc = hx[0:16, 0:128], hy[0:16, 0:128], hz[0:16, 0:128]
            ey, ez = fresh[1][0:16, 0:128], fresh[2][0:16, 0:128]
            terms = (
                (-math.cos(angle_h), hzc),
                (math.cos(angle_h), hyc),
                (math.cos(angle_e), ez),
                (-math.cos(angle_e), ey),
                (math.sin(angle_h), hzc),
                (-math.sin(angle_h), hyc),
                (-math.sin(angle_e), ez),
                (math.sin(angle_e), ey),
            )
            for o, (factor, value) in enumerate(terms):
                phasor_ref[o, x] = factor * value if n == 0 else phasor_ref[o, x] + factor * value
            if last:
                final_ref[3, x] = hxc
                final_ref[4, x] = hyc
                final_ref[5, x] = hzc

    copies = []
    for n in range(STEPS):
        planes = list(range(n - 4, 19 - n))
        states = {}
        for k in range(len(planes) + LAG):
            if k < len(planes):
                states[planes[k]] = magnetic_step(n, planes[k])
            if k >= LAG:
                x = planes[k - LAG]
                inner = 0 <= x < 16
                if inner or n < STEPS - 1:
                    electric_step(n, x, inner, *states.pop(x))
                if n == STEPS - 1 and inner and x % 4 == 3:
                    part = pl.ds(x - 3, 4)
                    copies.append(
                        pltpu.make_async_copy(
                            final_ref.at[:, part], out_ref.at[:, part], sems.at[x // 4]
                        )
                    )
                    copies[-1].start()

    count = ints_ref[72 + gz]

    def put_tile(t, carry):
        p = ints_ref[gz * SLOTS + t]
        live = jnp.where(t < count, 1.0, 0.0)
        rows = pl.ds(pl.multiple_of((p & 1) * 8, 8), 8)
        for o in range(8):
            cur_ref[pl.ds(pl.multiple_of(t * 64 + o * 8, 8), 8), :] = phasor_ref[o, p >> 1, rows, :] * live
        return carry

    lax.fori_loop(0, SLOTS, put_tile, 0)
    for copy in copies:
        copy.wait()


def kernel_options(mib):
    return pltpu.CompilerParams(vmem_limit_bytes=mib << 20)


def shift(block, axis, by):
    count = lax.axis_size(axis)
    pairs = [(i, i + by) for i in range(count) if 0 <= i + by < count]
    return lax.ppermute(block, axis, pairs)


def window(fields, polarization, material, medium, ints, sizes, dir_angles, dir_order):
    anywhere = pl.BlockSpec(memory_space=pl.ANY)
    depth = pl.pallas_call(
        pack_depth_kernel,
        out_shape=jax.ShapeDtypeStruct((13, 16, 128), HALO),
        in_specs=[pl.BlockSpec(memory_space=pltpu.HBM)] * 3,
        out_specs=whole(),
        scratch_shapes=[
            pltpu.VMEM((12, 16, 16, 128), jnp.float32),
            pltpu.VMEM((16, 16, 128), jnp.int32),
            pltpu.SemaphoreType.DMA((13,)),
        ],
        compiler_params=pltpu.CompilerParams(vmem_limit_bytes=65000 << 10),
        name="pack_depth",
    )(fields, polarization, material)
    later, _ = lax.optimization_barrier(((fields, polarization, material), depth))
    own = pl.pallas_call(
        stage_kernel,
        out_shape=jax.ShapeDtypeStruct((13, 16, 16, 128), jnp.float32),
        in_specs=[whole()] * 3,
        out_specs=whole(),
        compiler_params=kernel_options(6),
        name="stage",
    )(*later)
    before, after = shift(depth, "gz", 1), shift(depth, "gz", -1)
    low, high = pl.pallas_call(
        pack_x_kernel,
        out_shape=(
            jax.ShapeDtypeStruct((45, 16, 128), HALO),
            jax.ShapeDtypeStruct((48, 16, 128), HALO),
        ),
        in_specs=[whole()] * 3,
        out_specs=(whole(),) * 2,
        compiler_params=kernel_options(6),
        name="pack_x",
    )(own, before, after)
    left, right = shift(high, "gx", 1), shift(low, "gx", -1)
    u = directions(dir_angles, dir_order, low)
    half = tables(u, ints, low, 0)
    low, high = pl.pallas_call(
        pack_y_kernel,
        out_shape=(jax.ShapeDtypeStruct((13, 13, 8, 128), HALO),) * 2,
        in_specs=[whole()] * 5 + [anywhere],
        out_specs=(whole(),) * 2,
        compiler_params=kernel_options(6),
        name="pack_y",
    )(own, before, after, left, right, half[1])
    table, weight = tables(u, ints, low, 16, half)
    laid, laid_coef = pl.pallas_call(
        lay_kernel,
        out_shape=(
            jax.ShapeDtypeStruct((12, 24, 16, 256), jnp.float32),
            jax.ShapeDtypeStruct((4, 24, 16, 256), jnp.float32),
        ),
        in_specs=[scalars()] + [whole()] * 5 + [anywhere],
        out_specs=(whole(),) * 2,
        compiler_params=kernel_options(10),
        cost_estimate=pl.CostEstimate(flops=8000000, bytes_accessed=9000000, transcendentals=0),
        name="lay",
    )(medium, own, before, after, left, right, low)
    down, up = shift(high, "gy", 1), shift(low, "gy", -1)
    fields_out, currents = pl.pallas_call(
        functools.partial(window_kernel, sizes),
        out_shape=(
            jax.ShapeDtypeStruct((6, 16, 16, 128), jnp.float32),
            jax.ShapeDtypeStruct((SLOTS * 64, 128), jnp.float32),
        ),
        in_specs=[scalars()] * 2 + [whole()] * 4,
        out_specs=(anywhere, whole()),
        scratch_shapes=[
            pltpu.VMEM((12, 24, 24, 256), jnp.float32),
            pltpu.VMEM((12, 24, 8, 256), jnp.float32),
            pltpu.VMEM((4, 24, 8, 256), jnp.float32),
            pltpu.VMEM((8, 16, 16, 128), jnp.float32),
            pltpu.VMEM((6, 16, 16, 128), jnp.float32),
            pltpu.SemaphoreType.DMA((4,)),
        ],
        compiler_params=kernel_options(24),
        name="window",
    )(ints, medium, laid, laid_coef, down, up)
    return fields_out, currents, table, weight


TWO_PI = 2.0 * math.pi
TURN = 0.35 / TWO_PI
PAIRS = 4 * SLOTS


def sin_quarter(y):
    z = y * y
    c = [TWO_PI ** n * s / math.factorial(n) for n, s in ((1, 1), (3, -1), (5, 1), (7, -1), (9, 1), (11, -1))]
    acc = jnp.full_like(z, c[5])
    for k in (4, 3, 2, 1, 0):
        acc = acc * z + c[k]
    return acc * y


def cos_sin(turns):
    r = turns - jnp.floor(turns + 0.5)
    a = jnp.abs(r)
    cos = sin_quarter(0.25 - a)
    sin = sin_quarter(0.25 - jnp.abs(a - 0.25))
    return cos, jnp.where(r < 0, -sin, sin)


def dirs_kernel(angles_ref, order_ref, low_ref, u_ref):
    idx = order_ref[...]
    hi = idx >> 7
    lo = idx & 127

    def body(h, acc):
        polar, azim = acc
        pick = hi == h
        row_p = jnp.broadcast_to(angles_ref[0, pl.ds(h, 1), :], lo.shape)
        row_a = jnp.broadcast_to(angles_ref[1, pl.ds(h, 1), :], lo.shape)
        polar = jnp.where(pick, jnp.take_along_axis(row_p, lo, axis=1), polar)
        azim = jnp.where(pick, jnp.take_along_axis(row_a, lo, axis=1), azim)
        return polar, azim

    zero = jnp.zeros(idx.shape, jnp.float32)
    polar, azim = lax.fori_loop(0, 64, body, (zero, zero), unroll=16)
    cos_p, sin_p = cos_sin(polar * (1.0 / TWO_PI))
    cos_a, sin_a = cos_sin(azim * (1.0 / TWO_PI))
    u_ref[0] = sin_p * cos_a
    u_ref[1] = sin_p * sin_a
    u_ref[2] = cos_p


def directions(dir_angles, dir_order, low):
    order = dir_order.reshape(256, 32).T.reshape(64, 128)
    return pl.pallas_call(
        dirs_kernel,
        out_shape=jax.ShapeDtypeStruct((3, 64, 128), jnp.float32),
        in_specs=[whole(), whole(), pl.BlockSpec(memory_space=pl.ANY)],
        out_specs=whole(),
        cost_estimate=pl.CostEstimate(flops=3000000, bytes_accessed=300000, transcendentals=0),
        compiler_params=kernel_options(12),
        name="dirs",
    )(dir_angles.reshape(2, 64, 128), order, low)


def tables_kernel(first, ints_ref, low_ref, u_ref, *refs):
    table_ref, weight_ref, pos_ref = refs[-3:]

    @pl.when(pl.program_id(0) == 0)
    def _():
        gx, gy, gz = ints_ref[76], ints_ref[77], ints_ref[78]
        pos_ref[...] = jnp.zeros_like(pos_ref)
        for t in range(SLOTS):
            p = ints_ref[gz * SLOTS + t]
            for axis, start in enumerate((gx * 16 + (p >> 1), gy * 16 + (p & 1) * 8, gz * 128)):
                pos_ref[axis, t : t + 1, :] = jnp.full((1, 256), start.astype(jnp.float32))

    j2 = pl.multiple_of((pl.program_id(0) + first) * 2, 2)

    def row(axis):
        return jnp.concatenate(
            [u_ref[axis, pl.ds(j2, 1), :], u_ref[axis, pl.ds(j2 + 1, 1), :]], axis=1
        ) * TURN

    ux, uy, uz = row(0), row(1), row(2)
    eight = lax.broadcasted_iota(jnp.int32, (8, 256), 0).astype(jnp.float32)
    sixteen = lax.broadcasted_iota(jnp.int32, (16, 256), 0).astype(jnp.float32) * 8.0
    low_c, low_s = cos_sin(uz * eight)
    high_c, high_s = cos_sin(uz * sixteen)
    row_c, row_s = cos_sin(uy * eight)
    one_c, one_s = row_c[1:2], row_s[1:2]
    for pair in range(8):
        rows = ([], [], [], [])
        for half in range(2):
            a = 2 * pair + half
            hc, hs = high_c[a : a + 1], high_s[a : a + 1]
            c = hc * low_c - hs * low_s
            s = hs * low_c + hc * low_s
            rows[0].append(c)
            rows[1].append(c * one_c - s * one_s)
            rows[2].append(s)
            rows[3].append(s * one_c + c * one_s)
        for part in range(4):
            table_ref[0, part * 128 + 16 * pair : part * 128 + 16 * pair + 16, :] = jnp.concatenate(
                rows[part], axis=0
            ).astype(jnp.bfloat16)
    phase = pos_ref[0] * ux + pos_ref[1] * uy + pos_ref[2] * uz
    tile_c, tile_s = cos_sin(phase)
    for g in range(4):
        gc, gs = row_c[2 * g : 2 * g + 1], row_s[2 * g : 2 * g + 1]
        weight_ref[0, 0, 24 * g : 24 * g + 24, :] = tile_c * gc - tile_s * gs
        weight_ref[0, 1, 24 * g : 24 * g + 24, :] = tile_s * gc + tile_c * gs


def tables(u, ints, low, first, filled=()):
    anywhere = pl.BlockSpec(memory_space=pl.ANY)
    return pl.pallas_call(
        functools.partial(tables_kernel, first),
        grid=(16,),
        out_shape=(
            jax.ShapeDtypeStruct((32, 512, 256), jnp.bfloat16),
            jax.ShapeDtypeStruct((32, 2, 104, 256), jnp.float32),
        ),
        in_specs=[scalars(), anywhere, pl.BlockSpec((3, 64, 128), lambda j: (0, 0, 0))]
        + [anywhere] * len(filled),
        out_specs=(
            pl.BlockSpec((1, 512, 256), lambda j: (j + first, 0, 0)),
            pl.BlockSpec((1, 2, 104, 256), lambda j: (j + first, 0, 0, 0)),
        ),
        input_output_aliases={3 + k: k for k in range(len(filled))},
        scratch_shapes=[pltpu.VMEM((3, 24, 256), jnp.float32)],
        cost_estimate=pl.CostEstimate(flops=30000000, bytes_accessed=7000000, transcendentals=0),
        compiler_params=kernel_options(12),
        name="tables",
    )(ints, low, u, *filled)


def far_kernel(scale, cur_ref, table_ref, weight_ref, out_ref, lhs_ref, acc_ref, rows_ref):
    j = pl.program_id(0)

    @pl.when(j == 0)
    def _():
        sign = jnp.where(lax.broadcasted_iota(jnp.int32, (SLOTS * 8, 128), 0) % 8 < 4, -1.0, 1.0)
        for ty in range(8):
            g, half = ty // 2, ty % 2
            plain = cur_ref[pl.ds(ty, SLOTS * 8, stride=8), :]
            swapped = pltpu.roll(plain.reshape(SLOTS, 8, 128), 4, 1).reshape(SLOTS * 8, 128) * sign
            rows = slice(g * SLOTS * 8, (g + 1) * SLOTS * 8)
            lhs_ref[rows, half * 128 : half * 128 + 128] = plain.astype(jnp.bfloat16)
            lhs_ref[rows, 256 + half * 128 : 384 + half * 128] = swapped.astype(jnp.bfloat16)

    for k in range(PER_STEP):
        far_block(scale, j * PER_STEP + k, k, lhs_ref, table_ref, weight_ref, acc_ref)

    @pl.when(j == pl.num_programs(0) - 1)
    def _():
        turned = acc_ref[...].T
        rows_ref[pl.ds(0, 256, stride=2), :] = turned[:, 0:128]
        rows_ref[pl.ds(1, 256, stride=2), :] = turned[:, 128:256]
        out_ref[...] = rows_ref[...].astype(out_ref.dtype)


def far_block(scale, j, k, lhs_ref, table_ref, weight_ref, acc_ref):
    prod = jnp.dot(lhs_ref[...], table_ref[k], preferred_element_type=jnp.float32)
    first = jnp.zeros((8, 256), jnp.float32)
    second = jnp.zeros((8, 256), jnp.float32)
    for g in range(4):
        for t in range(SLOTS):
            row = 8 * (g * SLOTS + t)
            piece = prod[row : row + 8]
            first = first + piece * weight_ref[k, 0, pl.ds(24 * g + t, 8, stride=0), :]
            second = second + piece * weight_ref[k, 1, pl.ds(24 * g + t, 8, stride=0), :]
    sign = jnp.where(lax.broadcasted_iota(jnp.int32, (8, 256), 0) < 4, -scale, scale)
    acc_ref[pl.ds(pl.multiple_of(j * 8, 8), 8), :] = first * scale + pltpu.roll(second, 4, 0) * sign


def far_products(currents, table, weight, scale, dtype):
    return pl.pallas_call(
        functools.partial(far_kernel, scale),
        grid=(32 // PER_STEP,),
        out_shape=jax.ShapeDtypeStruct((512, 128), dtype),
        in_specs=[
            pl.BlockSpec((SLOTS * 64, 128), lambda j: (0, 0)),
            pl.BlockSpec((PER_STEP, 512, 256), lambda j: (j, 0, 0)),
            pl.BlockSpec((PER_STEP, 2, 104, 256), lambda j: (j, 0, 0, 0)),
        ],
        out_specs=pl.BlockSpec((512, 128), lambda j: (0, 0)),
        scratch_shapes=[
            pltpu.VMEM((4 * SLOTS * 8, 512), jnp.bfloat16),
            pltpu.VMEM((256, 256), jnp.float32),
            pltpu.VMEM((512, 128), jnp.float32),
        ],
        cost_estimate=pl.CostEstimate(flops=5000000000, bytes_accessed=15000000, transcendentals=0),
        compiler_params=kernel_options(12),
        name="far",
    )(currents, table, weight)


def sum_kernel(in_ref, out_ref):
    eight = jnp.sum(in_ref[...].astype(jnp.float32).reshape(64, 8, 128), axis=0)
    halves = [sum(eight[k : k + 1] for k in range(h + 2, 8, 2)) + eight[h : h + 1] for h in range(2)]
    total = jnp.concatenate(halves, axis=1)
    row = lax.broadcasted_iota(jnp.int32, (8, 256), 0)
    col = lax.broadcasted_iota(jnp.int32, (8, 256), 1) % 8
    spread = jnp.where((row % 2) * 4 + row // 2 == col, jnp.broadcast_to(total, (8, 256)), 0.0)
    pick = jnp.where(
        lax.broadcasted_iota(jnp.int32, (256, 32), 0) // 8
        == lax.broadcasted_iota(jnp.int32, (256, 32), 1),
        1.0,
        0.0,
    )
    out_ref[...] = jnp.dot(
        spread, pick, preferred_element_type=jnp.float32, precision=lax.Precision.HIGHEST
    )


def sum_sources(received):
    return pl.pallas_call(
        sum_kernel,
        out_shape=jax.ShapeDtypeStruct((8, 32), jnp.float32),
        in_specs=[whole()],
        out_specs=whole(),
        compiler_params=kernel_options(4),
        name="sum_sources",
    )(received).T


def shards(
    fields,
    polarization,
    material,
    omega0,
    damping,
    strength,
    tile_count,
    tile_place,
    dir_angles,
    dir_order,
):
    sizes = tuple(lax.axis_size(axis) * n for axis, n in zip(AXES, fields.shape[1:]))
    index = jnp.stack([lax.axis_index(axis) for axis in AXES]).astype(jnp.int32)
    ints = jnp.concatenate([tile_place.reshape(-1), tile_count.reshape(-1), index])
    medium = jnp.concatenate([omega0, damping, strength])
    fields_out, currents, table, weight = window(
        fields, polarization, material, medium, ints, sizes, dir_angles, dir_order
    )
    tile_total = math.prod(lax.axis_size(axis) for axis in AXES) * TILE_MEAN
    scale = 1.0 / math.sqrt(tile_total * TY * fields.shape[3])
    partial = far_products(currents, table, weight, scale, jnp.bfloat16)
    received = lax.all_to_all(partial, AXES, 0, 0, tiled=True)
    return fields_out, sum_sources(received)


def solution(mesh):
    return jax.shard_map(
        shards,
        mesh=mesh,
        in_specs=(
            P(None, *AXES),
            P(None, *AXES),
            P(*AXES),
            P(),
            P(),
            P(),
            P(("gx", "gy"), None),
            P(("gx", "gy"), None, None),
            P(),
            P(),
        ),
        out_specs=(P(None, *AXES), P(AXES, None)),
        check_vma=False,
    )
```
